128 devices in a mesh: depth: 8 (over x, y_lo), chan: 16 (over z, y_hi, core).
Axes of the slice: x: 4, y: 4 (y_hi: 2, y_lo: 2; y = y_hi * 2 + y_lo), z: 4, core: 2. Of those that a mesh axis runs over, the one named last changes fastest.
Arguments:
- volume: float32 [512, 32, 1024], P('chan', 'depth'), may hold values from -6 to 6
- conv_weight: float32 [1, 3, 16, 32, 864], P(None, None, 'chan'), may hold values from -0.21875 to 0.21875
- norm_gain: float32 [1, 512], replicated, may hold values from 0.1 to 1.9
- mlp_in: float32 [1, 1024, 512], replicated, may hold values from -0.25 to 0.25
- mlp_out: float32 [1, 512, 1024], replicated, may hold values from -0.1875 to 0.1875
Outputs:
- features: float32 [512, 32, 1024], P('chan', 'depth')
The draws below stay inside these ranges and needn't reach their ends.
All inputs are finite; a program needn't handle non-finite values.
Results may differ from the reference program's by a relative error of at most 0.0001.
Values sent between devices are 32-bit elements; how exact they have to be, the bound alone decides.
No kernel may reach another device: no remote copies, remote signals or barrier semaphores. Data moves between devices by JAX's collectives and lax.ppermute only.
A program may use at most 64 MiB of HBM per device.

```python
import jax
import jax.numpy as jnp
from jax import lax

C = 512
CG = 32
HID = 1024
H = 32
W = 32
BLOCKS = 1
CONVS = 3
GROUPS = 16
TAPS = 864
NZ = 32
HW = 1024


def block_scale(rng, dims, shards, least, top_value):
    gain = 1.0
    for position, parts in shards:
        draws = jax.random.uniform(jax.random.fold_in(jax.random.fold_in(rng, 6), position), (parts,), jnp.float32, least / len(shards), top_value / len(shards))
        gain = gain * jnp.repeat(jnp.exp(draws), dims[position] // parts).reshape((-1,) + (1,) * (len(dims) - 1 - position))
    return gain


def normal_values(rng, shape, deviation, bound, pieces=(), held_as=jnp.bfloat16):
    entries = deviation * jax.random.normal(rng, shape, jnp.float32)
    if pieces:
        entries = entries * block_scale(rng, shape, pieces, -0.22, 0.18)
    return jnp.clip(entries, -bound, bound).astype(held_as)


def setup_inputs(seed: int = 0) -> dict:
    keys = jax.random.split(jax.random.key(seed), 6)
    return {
        "volume": normal_values(keys[0], (C, NZ, HW), 1.0, 6.0, ((0, 16), (1, 8)), jnp.float32),
        "conv_weight": normal_values(keys[1], (BLOCKS, CONVS, GROUPS, CG, TAPS), TAPS ** -0.5, 0.21875, ((2, 16),), jnp.float32),
        "norm_gain": jnp.clip(1.0 + 0.18 * jax.random.normal(keys[2], (BLOCKS, C), jnp.float32), 0.1, 1.9),
        "mlp_in": normal_values(keys[3], (BLOCKS, HID, C), C ** -0.5, 0.25, (), jnp.float32),
        "mlp_out": normal_values(keys[4], (BLOCKS, C, HID), HID ** -0.5, 0.1875, (), jnp.float32),
    }


def convolve(field, kernel):
    grouped = field.reshape(GROUPS, CG, NZ, H, W)
    total = jnp.zeros_like(grouped)
    for shift_h in range(3):
        for shift_w in range(3):
            for shift_d in range(3):
                moved = jnp.roll(grouped, (1 - shift_d, 1 - shift_h, 1 - shift_w), (2, 3, 4))
                start = ((shift_h * 3 + shift_w) * 3 + shift_d) * CG
                piece = kernel[:, :, start:start + CG]
                total = total + jnp.einsum('goi,gizhw->gozhw', piece, moved, precision=lax.Precision.HIGHEST)
    return total.reshape(C, NZ, H * W)

def reference(volume, conv_weight, norm_gain, mlp_in, mlp_out):
    state = volume
    for block in range(BLOCKS):
        inner = jax.nn.gelu(convolve(state, conv_weight[block, 0]))
        inner = jax.nn.gelu(convolve(inner, conv_weight[block, 1]))
        mixed = state + convolve(inner, conv_weight[block, 2])
        flat = mixed.reshape(C, -1)
        scaled = flat * lax.rsqrt(lax.optimization_barrier(jnp.mean(flat * flat, axis=0)) + 1e-06) * norm_gain[block][:, None]
        hidden = jax.nn.gelu(jnp.dot(mlp_in[block], scaled, precision=lax.Precision.HIGHEST))
        flat = flat + jnp.dot(mlp_out[block], hidden, precision=lax.Precision.HIGHEST)
        state = flat.reshape(C, NZ, H * W)
    return state
```

```python
import functools

import jax
import jax.numpy as jnp
from jax import lax
from jax.experimental import pallas as pl
from jax.experimental.pallas import tpu as pltpu
from jax.sharding import PartitionSpec as P

W = 32
F32 = jnp.float32
BF16 = jnp.bfloat16
VMEM = pl.BlockSpec(memory_space=pltpu.VMEM)


def call(body, outs, flops, moved, n_in, scratch=(), limit=None):
    return pl.pallas_call(
        body,
        out_shape=outs,
        in_specs=[VMEM] * n_in,
        out_specs=jax.tree.map(lambda _: VMEM, outs),
        scratch_shapes=scratch,
        cost_estimate=pl.CostEstimate(flops=flops, bytes_accessed=moved, transcendentals=0),
        compiler_params=pltpu.CompilerParams(vmem_limit_bytes=limit or (32 << 20)),
    )


def halves(x):
    hi = x.astype(BF16)
    return hi, (x - hi.astype(F32)).astype(BF16)


def gelu(v):
    return 0.5 * v * (1.0 + jnp.tanh(0.7978845608028654 * (v + 0.044715 * (v * v * v))))


def planes_kernel(x_ref, lo_ref, mid_ref, hi_ref):
    lo_ref[...] = x_ref[:, 0, :]
    for p in range(mid_ref.shape[0]):
        mid_ref[p] = x_ref[:, p + 1, :]
    hi_ref[...] = x_ref[:, x_ref.shape[1] - 1, :]


def taps_kernel(k_ref, w_ref, pad_ref):
    layers, width, taps = k_ref.shape
    lane = lax.broadcasted_iota(jnp.int32, (width, 128), 1)
    pad_ref[...] = jnp.zeros_like(pad_ref)
    for layer in range(layers):
        pad_ref[:, :taps] = k_ref[layer]
        for tap in range(9):
            start = tap * 3 * width
            base, shift = start // 128 * 128, start % 128
            pair = pad_ref[:, base : base + 256]
            if shift:
                pair = pltpu.roll(pair, 256 - shift, 1)
            hi, lo = halves(jnp.where(lane < 3 * width, pair[:, :128], 0.0))
            rows = pl.ds(tap * width, width)
            w_ref[layer, rows, 0:128] = hi
            w_ref[layer, rows, 128:256] = hi
            w_ref[layer, rows, 256:384] = lo


def mlp_weights_kernel(gain_ref, a_ref, b_ref, ah_ref, al_ref, bh_ref, bl_ref):
    gain = gain_ref[...]
    rows = 128
    for r in range(0, a_ref.shape[0], rows):
        hi, lo = halves(a_ref[r : r + rows, :] * gain)
        ah_ref[r : r + rows, :] = hi
        al_ref[r : r + rows, :] = lo
    for r in range(0, b_ref.shape[0], rows):
        hi, lo = halves(b_ref[r : r + rows, :])
        bh_ref[r : r + rows, :] = hi
        bl_ref[r : r + rows, :] = lo


def conv_plane(weight, three, acc_ref):
    zero = jnp.zeros_like(three[0][0])
    his = [t[0] for t in three] + [zero]
    los = [t[1] for t in three] + [zero]
    acc_ref[...] = jnp.dot(weight, jnp.concatenate(his + los + his, axis=0), preferred_element_type=F32)
    width = zero.shape[0]
    cells = zero.shape[1]

    def tap(b, c):
        return acc_ref[(b * 3 + c) * width : (b * 3 + c + 1) * width, :]

    column = lax.broadcasted_iota(jnp.int32, (width, 128), 1) % W
    sums = [
        tap(1, c) + pltpu.roll(tap(0, c), W, 1) + pltpu.roll(tap(2, c), cells - W, 1) for c in range(3)
    ]
    parts = []
    for v in range(0, cells, 128):
        left, here, right = (s[:, v : v + 128] for s in sums)
        left = jnp.where(column == 0, pltpu.roll(left, 128 - W + 1, 1), pltpu.roll(left, 1, 1))
        right = jnp.where(column == W - 1, pltpu.roll(right, W - 1, 1), pltpu.roll(right, 127, 1))
        parts.append(left + here + right)
    return jnp.concatenate(parts, axis=1)


def inner_kernel(layer, last, w_ref, lo_ref, mid_ref, hi_ref, *rest):
    if last:
        base_ref, out_ref, acc_ref = rest
    else:
        out_ref, acc_ref = rest
    planes = [halves(lo_ref[...])] + [halves(mid_ref[p]) for p in range(mid_ref.shape[0])] + [halves(hi_ref[...])]
    weight = w_ref[layer]
    for p in range(mid_ref.shape[0]):
        total = conv_plane(weight, planes[p : p + 3], acc_ref.at[p])
        if last:
            store_cells(out_ref, p, base_ref[p] + total)
        else:
            out_ref[p] = gelu(total)


def store_cells(out_ref, plane, value):
    size = out_ref.shape[2]
    runs = value.shape[1] // size
    for q in range(runs):
        out_ref[plane * runs + q] = value[:, q * size : (q + 1) * size]


def outer_kernel(layer, last, w_ref, before_ref, lo_ref, mid_ref, hi_ref, after_ref, *rest):
    inner = mid_ref.shape[0]
    if last:
        base_lo_ref, base_hi_ref, done_ref, out_ref, acc_ref = rest
    else:
        out_lo_ref, out_hi_ref, acc_ref = rest
    weight = w_ref[layer]
    low = [halves(before_ref[...]), halves(lo_ref[...]), halves(mid_ref[0])]
    high = [halves(mid_ref[inner - 1]), halves(hi_ref[...]), halves(after_ref[...])]
    low = conv_plane(weight, low, acc_ref.at[0])
    if last:
        store_cells(out_ref, 0, base_lo_ref[...] + low)
    else:
        out_lo_ref[...] = gelu(low)
    high = conv_plane(weight, high, acc_ref.at[1])
    if last:
        store_cells(out_ref, inner + 1, base_hi_ref[...] + high)
        runs = done_ref.shape[0] // inner
        out_ref[runs : runs * (inner + 1)] = done_ref[...]
    else:
        out_hi_ref[...] = gelu(high)


def mlp_kernel(y_ref, ah_ref, al_ref, bh_ref, bl_ref, out_ref, hh_ref, hl_ref):
    y = y_ref[...]
    scale = lax.rsqrt(jnp.mean(y * y, axis=0, keepdims=True) + 1e-06)
    hi, lo = halves(y * scale)
    seen = jnp.concatenate([hi, lo, hi], axis=0)
    rows = 256
    for r in range(0, ah_ref.shape[0], rows):
        part = jnp.concatenate([ah_ref[r : r + rows, :], ah_ref[r : r + rows, :], al_ref[r : r + rows, :]], axis=1)
        hid = gelu(jnp.dot(part, seen, preferred_element_type=F32))
        hh, hl = halves(hid)
        hh_ref[r : r + rows, :] = hh
        hl_ref[r : r + rows, :] = hl
    seen = jnp.concatenate([hh_ref[...], hl_ref[...], hh_ref[...]], axis=0)
    for r in range(0, bh_ref.shape[0], rows):
        part = jnp.concatenate([bh_ref[r : r + rows, :], bh_ref[r : r + rows, :], bl_ref[r : r + rows, :]], axis=1)
        out_ref[r : r + rows, :] = y_ref[r : r + rows, :] + jnp.dot(part, seen, preferred_element_type=F32)


def place_kernel(in_ref, out_ref):
    size = in_ref.shape[2]
    runs = out_ref.shape[2] // size
    for p in range(out_ref.shape[1]):
        for q in range(runs):
            out_ref[:, p, q * size : (q + 1) * size] = in_ref[p * runs + q]


def per_device(volume, conv_weight, norm_gain, mlp_in, mlp_out):
    width, planes, cells = volume.shape
    inner = planes - 2
    count = lax.axis_size("depth")
    members = lax.axis_size("chan")
    kernels = conv_weight[0, :, 0]
    layers = kernels.shape[0]
    channels, hidden = mlp_out.shape[1], mlp_out.shape[2]
    size = planes * cells // members
    flops = 2 * 288 * 384 * cells
    plane = jax.ShapeDtypeStruct((width, cells), F32)
    middle = jax.ShapeDtypeStruct((inner, width, cells), F32)
    acc = [pltpu.VMEM((2, 9 * width, cells), F32)]
    up = [(i, (i + 1) % count) for i in range(count)]
    down = [((i + 1) % count, i) for i in range(count)]

    lo, mid, hi = call(planes_kernel, (plane, middle, plane), 0, volume.size * 8, 1)(volume)
    first = (lo, mid, hi)
    before = lax.ppermute(hi, "depth", up)
    after = lax.ppermute(lo, "depth", down)
    weight = call(
        taps_kernel,
        jax.ShapeDtypeStruct((layers, 9 * width, 384), BF16),
        0,
        kernels.size * 8,
        1,
        [pltpu.VMEM((width, 1024), F32)],
    )(kernels)
    w_in = jax.ShapeDtypeStruct((hidden, channels), BF16)
    w_out = jax.ShapeDtypeStruct((channels, hidden), BF16)
    pieces = call(
        mlp_weights_kernel, (w_in, w_in, w_out, w_out), 0, mlp_in.size * 16, 3
    )(norm_gain, mlp_in[0], mlp_out[0])
    for layer in range(layers):
        last = layer == layers - 1
        if last:
            done = call(
                functools.partial(inner_kernel, layer, True),
                jax.ShapeDtypeStruct((inner * cells // size, width, size), F32),
                inner * flops,
                volume.size * 8,
                5,
                acc,
            )(weight, lo, mid, hi, first[1])
            mixed = call(
                functools.partial(outer_kernel, layer, True),
                jax.ShapeDtypeStruct((members, width, size), F32),
                2 * flops,
                volume.size * 8,
                9,
                acc,
            )(weight, before, lo, mid, hi, after, first[0], first[2], done)
        else:
            new_mid = call(
                functools.partial(inner_kernel, layer, False), middle, inner * flops, volume.size * 8, 4, acc
            )(weight, lo, mid, hi)
            new_lo, new_hi = call(
                functools.partial(outer_kernel, layer, False), (plane, plane), 2 * flops, volume.size * 8, 6, acc
            )(weight, before, lo, mid, hi, after)
            lo, mid, hi = new_lo, new_mid, new_hi
            before = lax.ppermute(hi, "depth", up)
            after = lax.ppermute(lo, "depth", down)
    here = lax.all_to_all(mixed, "chan", split_axis=0, concat_axis=0, tiled=True)
    out = call(
        mlp_kernel,
        jax.ShapeDtypeStruct((channels, size), F32),
        12 * hidden * channels * size,
        mlp_in.size * 8,
        5,
        [pltpu.VMEM((hidden, size), BF16)] * 2,
    )(here.reshape(channels, size), *pieces)
    back = lax.all_to_all(out.reshape(members, width, size), "chan", split_axis=0, concat_axis=0, tiled=True)
    return call(place_kernel, jax.ShapeDtypeStruct(volume.shape, F32), 0, volume.size * 8, 1)(back)


def solution(mesh):
    in_specs = (P("chan", "depth", None), P(None, None, "chan", None, None), P(), P(), P())
    out_specs = P("chan", "depth", None)
    return jax.shard_map(
        per_device, mesh=mesh, in_specs=in_specs, out_specs=out_specs, check_vma=False
    )
```

```python
import functools

import jax
import jax.numpy as jnp
from jax import lax
from jax.experimental import pallas as pl
from jax.experimental.pallas import tpu as pltpu
from jax.sharding import PartitionSpec as P

W = 32
F32 = jnp.float32
BF16 = jnp.bfloat16
VMEM = pl.BlockSpec(memory_space=pltpu.VMEM)
HBM = pl.BlockSpec(memory_space=pltpu.HBM)


def call(body, outs, flops, moved, ins, scratch=(), outs_in=VMEM, room=32 << 20):
    return pl.pallas_call(
        body,
        out_shape=outs,
        in_specs=ins,
        out_specs=jax.tree.map(lambda _: outs_in, outs),
        scratch_shapes=scratch,
        cost_estimate=pl.CostEstimate(flops=flops, bytes_accessed=moved, transcendentals=0),
        compiler_params=pltpu.CompilerParams(vmem_limit_bytes=room),
    )


def halves(x):
    hi = x.astype(BF16)
    return hi, (x - hi.astype(F32)).astype(BF16)


def gelu(v):
    return 0.5 * v * (1.0 + jnp.tanh(0.7978845608028654 * (v + 0.044715 * (v * v * v))))


def turned_here():
    return lax.axis_index("depth") % 2 > 0


def planes_kernel(x_ref, *q_refs):
    last = len(q_refs) - 1
    flip = turned_here()
    for k, q_ref in enumerate(q_refs):
        q_ref[...] = jnp.where(flip, x_ref[:, last - k, :], x_ref[:, k, :])


def taps_kernel(k_ref, w_ref, pad_ref):
    layers, width, taps = k_ref.shape
    flip = turned_here()
    lane = lax.broadcasted_iota(jnp.int32, (width, 128), 1)
    pad_ref[...] = jnp.zeros_like(pad_ref)
    for layer in range(layers):
        pad_ref[:, :taps] = k_ref[layer]
        for tap in range(9):
            start = tap * 3 * width
            base, shift = start // 128 * 128, start % 128
            pair = pad_ref[:, base : base + 256]
            if shift:
                pair = pltpu.roll(pair, 256 - shift, 1)
            ahead = pair[:, :128]
            turned = jnp.where(
                lane < width,
                pltpu.roll(ahead, 128 - 2 * width, 1),
                jnp.where(lane < 2 * width, ahead, pltpu.roll(ahead, 2 * width, 1)),
            )
            hi, lo = halves(jnp.where(lane < 3 * width, jnp.where(flip, turned, ahead), 0.0))
            rows = pl.ds(tap * width, width)
            w_ref[layer, rows, 0:128] = hi
            w_ref[layer, rows, 128:256] = hi
            w_ref[layer, rows, 256:384] = lo


def mlp_weights_kernel(gain_ref, a_ref, b_ref, w_hbm, w_ref, sems):
    gain = gain_ref[...]
    hidden, channels = a_ref.shape
    rows = 128
    copies = []

    def send(start, count):
        part = pl.ds(start, count)
        copies.append(pltpu.make_async_copy(w_ref.at[part], w_hbm.at[part], sems.at[len(copies)]))
        copies[-1].start()

    for r in range(0, hidden, rows):
        hi, lo = halves(a_ref[r : r + rows, :] * gain)
        w_ref[r : r + rows, :] = hi
        w_ref[hidden + r : hidden + r + rows, :] = lo
    send(0, 2 * hidden)
    base = 2 * hidden
    for half in range(hidden // channels):
        for r in range(0, channels, rows):
            hi, lo = halves(b_ref[r : r + rows, half * channels : (half + 1) * channels])
            at = base + half * channels + r
            w_ref[at : at + rows, :] = hi
            w_ref[at + hidden : at + hidden + rows, :] = lo
    send(base, 2 * hidden)
    for copy in copies:
        copy.wait()


def conv_plane(weight, three, acc_ref):
    zero = jnp.zeros_like(three[0][0])
    his = [t[0] for t in three] + [zero]
    los = [t[1] for t in three] + [zero]
    acc_ref[...] = jnp.dot(weight, jnp.concatenate(his + los + his, axis=0), preferred_element_type=F32)
    width = zero.shape[0]
    cells = zero.shape[1]

    def tap(b, c):
        return acc_ref[(b * 3 + c) * width : (b * 3 + c + 1) * width, :]

    column = lax.broadcasted_iota(jnp.int32, (width, 128), 1) % W
    sums = [
        tap(1, c) + pltpu.roll(tap(0, c), W, 1) + pltpu.roll(tap(2, c), cells - W, 1) for c in range(3)
    ]
    parts = []
    for v in range(0, cells, 128):
        left, here, right = (s[:, v : v + 128] for s in sums)
        left = jnp.where(column == 0, pltpu.roll(left, 128 - W + 1, 1), pltpu.roll(left, 1, 1))
        right = jnp.where(column == W - 1, pltpu.roll(right, W - 1, 1), pltpu.roll(right, 127, 1))
        parts.append(left + here + right)
    return jnp.concatenate(parts, axis=1)


def store_cells(out_ref, plane, value):
    size = out_ref.shape[2]
    runs = value.shape[1] // size
    for q in range(runs):
        out_ref[plane * runs + q] = value[:, q * size : (q + 1) * size]


def stage_kernel(given, work, kept, first, w_ref, *refs):
    ins, refs = refs[: len(given)], refs[len(given) :]
    acc_ref = refs[-1]
    layers = w_ref.shape[0]
    ends = any(layer == layers for layer, _ in work)
    done_ref = refs[0] if len(refs) > len(kept) + ends + 1 else None
    refs = refs[done_ref is not None :]
    where = dict(zip(given, ins, strict=True))
    kept_at = dict(zip(kept, refs[: len(kept)], strict=True))
    held = {key: halves(ref[...]) for key, ref in where.items()}
    for n, (layer, place) in enumerate(work):
        total = conv_plane(w_ref[layer - 1], [held[layer - 1, place + d] for d in (-1, 0, 1)], acc_ref.at[n % 2])
        if layer == layers:
            store_cells(refs[len(kept)], place - first, where[0, place][...] + total)
            continue
        total = gelu(total)
        held[layer, place] = halves(total)
        if (layer, place) in kept_at:
            kept_at[layer, place][...] = total
    if done_ref is not None:
        out_ref = refs[len(kept)]
        out_ref[out_ref.shape[0] - done_ref.shape[0] :] = done_ref[...]


def mlp_kernel(y_ref, w_hbm, out_ref, w_ref, hh_ref, hl_ref, sems):
    channels = y_ref.shape[0]
    hidden = hh_ref.shape[0]
    rows = 256
    copies = []

    def fetch(*starts):
        group = []
        for start in starts:
            part = pl.ds(start, rows)
            group.append(pltpu.make_async_copy(w_hbm.at[part], w_ref.at[part], sems.at[len(copies) * 8 + len(group)]))
            group[-1].start()
        copies.append(group)

    base = 2 * hidden
    for r in range(0, hidden, rows):
        fetch(r, hidden + r)
    for r in range(0, channels, rows):
        fetch(*(base + part * channels + r for part in range(2 * hidden // channels)))
    y = y_ref[...]
    scale = lax.rsqrt(jnp.mean(y * y, axis=0, keepdims=True) + 1e-06)
    hi, lo = halves(y * scale)
    seen = jnp.concatenate([hi, lo, hi], axis=0)
    for n, r in enumerate(range(0, hidden, rows)):
        for copy in copies[n]:
            copy.wait()
        top, low = w_ref[r : r + rows, :], w_ref[hidden + r : hidden + r + rows, :]
        hid = gelu(jnp.dot(jnp.concatenate([top, top, low], axis=1), seen, preferred_element_type=F32))
        hh, hl = halves(hid)
        hh_ref[r : r + rows, :] = hh
        hl_ref[r : r + rows, :] = hl
    seen = jnp.concatenate([hh_ref[...], hl_ref[...], hh_ref[...]], axis=0)
    for n, r in enumerate(range(0, channels, rows)):
        for copy in copies[hidden // rows + n]:
            copy.wait()
        parts = [w_ref[base + p * channels + r : base + p * channels + r + rows, :] for p in range(2 * hidden // channels)]
        top = parts[: hidden // channels]
        part = jnp.concatenate(top + top + parts[hidden // channels :], axis=1)
        out_ref[r : r + rows, :] = y_ref[r : r + rows, :] + jnp.dot(part, seen, preferred_element_type=F32)


def place_kernel(in_ref, out_ref):
    size = in_ref.shape[2]
    runs = out_ref.shape[2] // size
    last = out_ref.shape[1] - 1
    flip = turned_here()
    for p in range(last + 1):
        for q in range(runs):
            out_ref[:, p, q * size : (q + 1) * size] = jnp.where(
                flip, in_ref[(last - p) * runs + q], in_ref[p * runs + q]
            )

def per_device(volume, conv_weight, norm_gain, mlp_in, mlp_out):
    width, planes, cells = volume.shape
    count = lax.axis_size("depth")
    members = lax.axis_size("chan")
    kernels = conv_weight[0, :, 0]
    layers = kernels.shape[0]
    channels, hidden = mlp_out.shape[1], mlp_out.shape[2]
    size = planes * cells // members
    runs = cells // size
    plane = jax.ShapeDtypeStruct((width, cells), F32)

    pair = [(i, i ^ 1) for i in range(count)]
    along = [(i, (i + (2 if i % 2 == 0 else count - 2)) % count) for i in range(count)]
    own = call(planes_kernel, (plane,) * planes, 0, volume.size * 8, [VMEM])(volume)
    there = [lax.ppermute(q, "depth", pair) for q in own[:2]]
    taps = call(
        taps_kernel,
        jax.ShapeDtypeStruct((layers, 9 * width, 384), BF16),
        0,
        kernels.size * 8,
        [VMEM],
        [pltpu.VMEM((width, 1024), F32)],
    )(kernels)
    held = {(0, 3 + k): v for k, v in enumerate(own)}

    def stage(given, work, kept, finished=None, placed=0, first=0):
        outs = (plane,) * len(kept)
        if placed:
            outs += (jax.ShapeDtypeStruct((placed * runs, width, size), F32),)
        more = [] if finished is None else [finished]
        got = call(
            functools.partial(stage_kernel, given, work, kept, first),
            outs,
            len(work) * 2 * 288 * 384 * cells,
            (len(given) + len(outs)) * width * cells * 4,
            [VMEM] * (1 + len(given) + len(more)),
            [pltpu.VMEM((2, 9 * width, cells), F32)],
        )(taps, *[held[key] for key in given], *more)
        held.update(zip(kept, got))
        return got[-1]

    stage(((0, 3), (0, 4), (0, 5), (0, 6)), ((1, 4), (1, 5)), ((1, 4), (1, 5)))
    third, held[1, 4], held[1, 5] = lax.optimization_barrier((own[2], held[1, 4], held[1, 5]))
    there += [lax.ppermute(q, "depth", pair) for q in (third, own[3])]
    for k in range(layers):
        held[0, 2 - k] = lax.ppermute(there[k], "depth", along)
        held[0, 9 - k] = there[k + 1]
    stage(
        ((0, 1), (0, 2), (0, 3), (0, 4), (1, 4), (1, 5)),
        ((1, 3), (1, 2), (2, 4), (2, 3)),
        ((1, 2), (1, 3), (2, 3), (2, 4)),
    )
    most = stage(
        ((0, 4), (0, 5), (0, 6), (0, 7), (0, 8), (0, 9), (1, 4), (1, 5), (2, 3), (2, 4)),
        ((1, 6), (1, 7), (1, 8), (2, 5), (2, 6), (2, 7), (3, 4), (3, 5), (3, 6)),
        (),
        placed=3,
        first=4,
    )
    mixed = stage(
        ((0, 0), (0, 1), (0, 2), (0, 3), (1, 2), (1, 3), (2, 3), (2, 4)),
        ((1, 1), (2, 2), (3, 3)),
        (),
        finished=most,
        placed=4,
        first=3,
    )
    pieces = call(
        mlp_weights_kernel,
        jax.ShapeDtypeStruct((4 * hidden, channels), BF16),
        0,
        mlp_in.size * 16,
        [VMEM] * 3,
        [pltpu.VMEM((4 * hidden, channels), BF16), pltpu.SemaphoreType.DMA((2,))],
        HBM,
        52 << 20,
    )(norm_gain, mlp_in[0], mlp_out[0])

    here = lax.all_to_all(mixed, "chan", split_axis=0, concat_axis=0, tiled=True)
    out = call(
        mlp_kernel,
        jax.ShapeDtypeStruct((channels, size), F32),
        12 * hidden * channels * size,
        mlp_in.size * 8,
        [VMEM, HBM],
        [
            pltpu.VMEM((4 * hidden, channels), BF16),
            pltpu.VMEM((hidden, size), BF16),
            pltpu.VMEM((hidden, size), BF16),
            pltpu.SemaphoreType.DMA((64,)),
        ],
        room=52 << 20,
    )(here.reshape(channels, size), pieces)
    back = lax.all_to_all(out.reshape(members, width, size), "chan", split_axis=0, concat_axis=0, tiled=True)
    return call(place_kernel, jax.ShapeDtypeStruct(volume.shape, F32), 0, volume.size * 8, [VMEM])(back)


def solution(mesh):
    in_specs = (P("chan", "depth", None), P(None, None, "chan", None, None), P(), P(), P())
    out_specs = P("chan", "depth", None)
    return jax.shard_map(
        per_device, mesh=mesh, in_specs=in_specs, out_specs=out_specs, check_vma=False
    )
```

```python
import functools

import jax
import jax.numpy as jnp
from jax import lax
from jax.experimental import pallas as pl
from jax.experimental.pallas import tpu as pltpu
from jax.sharding import PartitionSpec as P

W = 32
F32 = jnp.float32
BF16 = jnp.bfloat16
VMEM = pl.BlockSpec(memory_space=pltpu.VMEM)


def call(body, outs, flops, moved, ins, scratch=()):
    return pl.pallas_call(
        body,
        out_shape=outs,
        in_specs=ins,
        out_specs=jax.tree.map(lambda _: VMEM, outs),
        scratch_shapes=scratch,
        cost_estimate=pl.CostEstimate(flops=flops, bytes_accessed=moved, transcendentals=0),
        compiler_params=pltpu.CompilerParams(vmem_limit_bytes=32 << 20),
    )


def halves(x):
    hi = x.astype(BF16)
    return hi, (x - hi.astype(F32)).astype(BF16)


def gelu(v):
    return 0.5 * v * (1.0 + jnp.tanh(0.7978845608028654 * (v + 0.044715 * (v * v * v))))


def turned_here():
    return lax.axis_index("depth") % 2 > 0


def planes_kernel(x_ref, *q_refs):
    last = len(q_refs) - 1
    flip = turned_here()
    for k, q_ref in enumerate(q_refs):
        q_ref[...] = jnp.where(flip, x_ref[:, last - k, :], x_ref[:, k, :])


def taps_kernel(k_ref, w_ref, pad_ref):
    layers, width, taps = k_ref.shape
    flip = turned_here()
    lane = lax.broadcasted_iota(jnp.int32, (width, 128), 1)
    pad_ref[...] = jnp.zeros_like(pad_ref)
    for layer in range(layers):
        pad_ref[:, :taps] = k_ref[layer]
        for tap in range(9):
            start = tap * 3 * width
            base, shift = start // 128 * 128, start % 128
            pair = pad_ref[:, base : base + 256]
            if shift:
                pair = pltpu.roll(pair, 256 - shift, 1)
            ahead = pair[:, :128]
            turned = jnp.where(
                lane < width,
                pltpu.roll(ahead, 128 - 2 * width, 1),
                jnp.where(lane < 2 * width, ahead, pltpu.roll(ahead, 2 * width, 1)),
            )
            hi, lo = halves(jnp.where(lane < 3 * width, jnp.where(flip, turned, ahead), 0.0))
            rows = pl.ds(tap * width, width)
            w_ref[layer, rows, 0:128] = hi
            w_ref[layer, rows, 128:256] = hi
            w_ref[layer, rows, 256:384] = lo


def mlp_weights_kernel(gain_ref, a_ref, b_ref, w_ref):
    gain = gain_ref[...]
    hidden, channels = a_ref.shape
    rows = 128
    for r in range(0, hidden, rows):
        hi, lo = halves(a_ref[r : r + rows, :] * gain)
        w_ref[r : r + rows, :] = hi
        w_ref[hidden + r : hidden + r + rows, :] = lo
    base = 2 * hidden
    for half in range(hidden // channels):
        for r in range(0, channels, rows):
            hi, lo = halves(b_ref[r : r + rows, half * channels : (half + 1) * channels])
            at = base + half * channels + r
            w_ref[at : at + rows, :] = hi
            w_ref[at + hidden : at + hidden + rows, :] = lo


def conv_plane(weight, three, acc_ref):
    zero = jnp.zeros_like(three[0][0])
    his = [t[0] for t in three] + [zero]
    los = [t[1] for t in three] + [zero]
    acc_ref[...] = jnp.dot(weight, jnp.concatenate(his + los + his, axis=0), preferred_element_type=F32)
    width = zero.shape[0]
    cells = zero.shape[1]

    def tap(b, c):
        return acc_ref[(b * 3 + c) * width : (b * 3 + c + 1) * width, :]

    column = lax.broadcasted_iota(jnp.int32, (width, 128), 1) % W
    sums = [
        tap(1, c) + pltpu.roll(tap(0, c), W, 1) + pltpu.roll(tap(2, c), cells - W, 1) for c in range(3)
    ]
    parts = []
    for v in range(0, cells, 128):
        left, here, right = (s[:, v : v + 128] for s in sums)
        left = jnp.where(column == 0, pltpu.roll(left, 128 - W + 1, 1), pltpu.roll(left, 1, 1))
        right = jnp.where(column == W - 1, pltpu.roll(right, W - 1, 1), pltpu.roll(right, 127, 1))
        parts.append(left + here + right)
    return jnp.concatenate(parts, axis=1)


def store_cells(out_ref, plane, value):
    size = out_ref.shape[2]
    runs = value.shape[1] // size
    for q in range(runs):
        out_ref[plane * runs + q] = value[:, q * size : (q + 1) * size]


def stage_kernel(given, work, kept, first, w_ref, *refs):
    ins, refs = refs[: len(given)], refs[len(given) :]
    acc_ref = refs[-1]
    layers = w_ref.shape[0]
    ends = any(layer == layers for layer, _ in work)
    done_ref = refs[0] if len(refs) > len(kept) + ends + 1 else None
    refs = refs[done_ref is not None :]
    where = dict(zip(given, ins, strict=True))
    kept_at = dict(zip(kept, refs[: len(kept)], strict=True))
    held = {key: halves(ref[...]) for key, ref in where.items()}
    for n, (layer, place) in enumerate(work):
        total = conv_plane(w_ref[layer - 1], [held[layer - 1, place + d] for d in (-1, 0, 1)], acc_ref.at[n % 2])
        if layer == layers:
            store_cells(refs[len(kept)], place - first, where[0, place][...] + total)
            continue
        total = gelu(total)
        held[layer, place] = halves(total)
        if (layer, place) in kept_at:
            kept_at[layer, place][...] = total
    if done_ref is not None:
        out_ref = refs[len(kept)]
        out_ref[out_ref.shape[0] - done_ref.shape[0] :] = done_ref[...]


def mlp_kernel(y_ref, w_ref, out_ref, hh_ref, hl_ref):
    channels = y_ref.shape[0]
    hidden = hh_ref.shape[0]
    rows = 256
    base = 2 * hidden
    y = y_ref[...]
    scale = lax.rsqrt(jnp.mean(y * y, axis=0, keepdims=True) + 1e-06)
    hi, lo = halves(y * scale)
    seen = jnp.concatenate([hi, lo, hi], axis=0)
    for r in range(0, hidden, rows):
        top, low = w_ref[r : r + rows, :], w_ref[hidden + r : hidden + r + rows, :]
        hid = gelu(jnp.dot(jnp.concatenate([top, top, low], axis=1), seen, preferred_element_type=F32))
        hh, hl = halves(hid)
        hh_ref[r : r + rows, :] = hh
        hl_ref[r : r + rows, :] = hl
    seen = jnp.concatenate([hh_ref[...], hl_ref[...], hh_ref[...]], axis=0)
    for r in range(0, channels, rows):
        parts = [w_ref[base + p * channels + r : base + p * channels + r + rows, :] for p in range(2 * hidden // channels)]
        top = parts[: hidden // channels]
        part = jnp.concatenate(top + top + parts[hidden // channels :], axis=1)
        out_ref[r : r + rows, :] = y_ref[r : r + rows, :] + jnp.dot(part, seen, preferred_element_type=F32)


def place_kernel(in_ref, out_ref):
    size = in_ref.shape[2]
    runs = out_ref.shape[2] // size
    last = out_ref.shape[1] - 1
    flip = turned_here()
    for p in range(last + 1):
        for q in range(runs):
            out_ref[:, p, q * size : (q + 1) * size] = jnp.where(
                flip, in_ref[(last - p) * runs + q], in_ref[p * runs + q]
            )

def per_device(volume, conv_weight, norm_gain, mlp_in, mlp_out):
    width, planes, cells = volume.shape
    count = lax.axis_size("depth")
    members = lax.axis_size("chan")
    kernels = conv_weight[0, :, 0]
    layers = kernels.shape[0]
    channels, hidden = mlp_out.shape[1], mlp_out.shape[2]
    size = planes * cells // members
    runs = cells // size
    plane = jax.ShapeDtypeStruct((width, cells), F32)

    pair = [(i, i ^ 1) for i in range(count)]
    along = [(i, (i + (2 if i % 2 == 0 else count - 2)) % count) for i in range(count)]
    own = call(planes_kernel, (plane,) * planes, 0, volume.size * 8, [VMEM])(volume)
    there = [lax.ppermute(q, "depth", pair) for q in own[:2]]
    taps = call(
        taps_kernel,
        jax.ShapeDtypeStruct((layers, 9 * width, 384), BF16),
        0,
        kernels.size * 8,
        [VMEM],
        [pltpu.VMEM((width, 1024), F32)],
    )(kernels)
    held = {(0, 3 + k): v for k, v in enumerate(own)}

    def stage(given, work, kept, finished=None, placed=0, first=0):
        outs = (plane,) * len(kept)
        if placed:
            outs += (jax.ShapeDtypeStruct((placed * runs, width, size), F32),)
        more = [] if finished is None else [finished]
        got = call(
            functools.partial(stage_kernel, given, work, kept, first),
            outs,
            len(work) * 2 * 288 * 384 * cells,
            (len(given) + len(outs)) * width * cells * 4,
            [VMEM] * (1 + len(given) + len(more)),
            [pltpu.VMEM((2, 9 * width, cells), F32)],
        )(taps, *[held[key] for key in given], *more)
        held.update(zip(kept, got))
        return got[-1]

    stage(((0, 3), (0, 4), (0, 5), (0, 6)), ((1, 4), (1, 5)), ((1, 4), (1, 5)))
    third, held[1, 4], held[1, 5] = lax.optimization_barrier((own[2], held[1, 4], held[1, 5]))
    there += [lax.ppermute(q, "depth", pair) for q in (third, own[3])]
    for k in range(layers):
        held[0, 2 - k] = lax.ppermute(there[k], "depth", along)
        held[0, 9 - k] = there[k + 1]
    pieces = call(
        mlp_weights_kernel,
        jax.ShapeDtypeStruct((4 * hidden, channels), BF16),
        0,
        mlp_in.size * 16,
        [VMEM] * 3,
    )(norm_gain, mlp_in[0], mlp_out[0])
    pieces, held[1, 4] = lax.optimization_barrier((pieces, held[1, 4]))
    stage(
        ((0, 1), (0, 2), (0, 3), (0, 4), (1, 4), (1, 5)),
        ((1, 3), (1, 2), (2, 4), (2, 3)),
        ((1, 2), (1, 3), (2, 3), (2, 4)),
    )
    most = stage(
        ((0, 4), (0, 5), (0, 6), (0, 7), (0, 8), (0, 9), (1, 4), (1, 5), (2, 3), (2, 4)),
        ((1, 6), (1, 7), (1, 8), (2, 5), (2, 6), (2, 7), (3, 4), (3, 5), (3, 6)),
        (),
        placed=3,
        first=4,
    )
    mixed = stage(
        ((0, 0), (0, 1), (0, 2), (0, 3), (1, 2), (1, 3), (2, 3), (2, 4)),
        ((1, 1), (2, 2), (3, 3)),
        (),
        finished=most,
        placed=4,
        first=3,
    )
    here = lax.all_to_all(mixed, "chan", split_axis=0, concat_axis=0, tiled=True)
    out = call(
        mlp_kernel,
        jax.ShapeDtypeStruct((channels, size), F32),
        12 * hidden * channels * size,
        mlp_in.size * 8,
        [VMEM, VMEM],
        [pltpu.VMEM((hidden, size), BF16)] * 2,
    )(here.reshape(channels, size), pieces)
    back = lax.all_to_all(out.reshape(members, width, size), "chan", split_axis=0, concat_axis=0, tiled=True)
    return call(place_kernel, jax.ShapeDtypeStruct(volume.shape, F32), 0, volume.size * 8, [VMEM])(back)


def solution(mesh):
    in_specs = (P("chan", "depth", None), P(None, None, "chan", None, None), P(), P(), P())
    out_specs = P("chan", "depth", None)
    return jax.shard_map(
        per_device, mesh=mesh, in_specs=in_specs, out_specs=out_specs, check_vma=False
    )
```

```python
import functools

import jax
import jax.numpy as jnp
from jax import lax
from jax.experimental import pallas as pl
from jax.experimental.pallas import tpu as pltpu
from jax.sharding import PartitionSpec as P

W = 32
F32 = jnp.float32
BF16 = jnp.bfloat16
VMEM = pl.BlockSpec(memory_space=pltpu.VMEM)


def call(body, outs, flops, moved, ins, scratch=(), aliases=None):
    return pl.pallas_call(
        body,
        out_shape=outs,
        in_specs=ins,
        out_specs=jax.tree.map(lambda _: VMEM, outs),
        scratch_shapes=scratch,
        input_output_aliases=aliases or {},
        cost_estimate=pl.CostEstimate(flops=flops, bytes_accessed=moved, transcendentals=0),
        compiler_params=pltpu.CompilerParams(vmem_limit_bytes=32 << 20),
    )


def halves(x):
    hi = x.astype(BF16)
    return hi, (x - hi.astype(F32)).astype(BF16)


def gelu(v):
    return 0.5 * v * (1.0 + jnp.tanh(0.7978845608028654 * (v + 0.044715 * (v * v * v))))


def turned_here():
    return lax.axis_index("depth") % 2 > 0


def planes_kernel(x_ref, *q_refs):
    last = len(q_refs) - 1
    flip = turned_here()
    for k, q_ref in enumerate(q_refs):
        q_ref[...] = jnp.where(flip, x_ref[:, last - k, :], x_ref[:, k, :])


def taps_kernel(k_ref, w_ref, pad_ref):
    layers, width, taps = k_ref.shape
    flip = turned_here()
    lane = lax.broadcasted_iota(jnp.int32, (width, 128), 1)
    pad_ref[...] = jnp.zeros_like(pad_ref)
    for layer in range(layers):
        pad_ref[:, :taps] = k_ref[layer]
        for tap in range(9):
            start = tap * 3 * width
            base, shift = start // 128 * 128, start % 128
            pair = pad_ref[:, base : base + 256]
            if shift:
                pair = pltpu.roll(pair, 256 - shift, 1)
            ahead = pair[:, :128]
            turned = jnp.where(lane // width == 1, ahead, pltpu.roll(ahead, 2 * width, 1))
            hi, lo = halves(jnp.where(lane < 3 * width, jnp.where(flip, turned, ahead), 0.0))
            rows = pl.ds(tap * width, width)
            w_ref[layer, rows, 0:128] = hi
            w_ref[layer, rows, 128:256] = hi
            w_ref[layer, rows, 256:384] = lo


def first_weights_kernel(gain_ref, a_ref, w_ref):
    gain = gain_ref[...]
    hidden = a_ref.shape[0]
    rows = 128
    for r in range(0, hidden, rows):
        hi, lo = halves(a_ref[r : r + rows, :] * gain)
        w_ref[r : r + rows, :] = hi
        w_ref[hidden + r : hidden + r + rows, :] = lo


def second_weights_kernel(b_ref, w_ref):
    channels = b_ref.shape[0]
    rows = 128
    for r in range(0, channels, rows):
        hi, lo = halves(b_ref[r : r + rows, :])
        w_ref[r : r + rows, :] = hi
        w_ref[channels + r : channels + r + rows, :] = lo


def conv_plane(weight, three, acc_ref):
    zero = jnp.zeros_like(three[0][0])
    his = [t[0] for t in three] + [zero]
    los = [t[1] for t in three] + [zero]
    acc_ref[...] = jnp.dot(weight, jnp.concatenate(his + los + his, axis=0), preferred_element_type=F32)
    width = zero.shape[0]
    cells = zero.shape[1]

    def tap(b, c):
        return acc_ref[(b * 3 + c) * width : (b * 3 + c + 1) * width, :]

    column = lax.broadcasted_iota(jnp.int32, (width, 128), 1) % W
    sums = [
        tap(1, c) + pltpu.roll(tap(0, c), W, 1) + pltpu.roll(tap(2, c), cells - W, 1) for c in range(3)
    ]
    parts = []
    for v in range(0, cells, 128):
        left, here, right = (s[:, v : v + 128] for s in sums)
        left = jnp.where(column == 0, pltpu.roll(left, 128 - W + 1, 1), pltpu.roll(left, 1, 1))
        right = jnp.where(column == W - 1, pltpu.roll(right, W - 1, 1), pltpu.roll(right, 127, 1))
        parts.append(left + here + right)
    return jnp.concatenate(parts, axis=1)


def store_cells(out_ref, plane, value):
    size = out_ref.shape[2]
    runs = value.shape[1] // size
    for q in range(runs):
        out_ref[plane * runs + q] = value[:, q * size : (q + 1) * size]


def stage_kernel(given, work, kept, first, resumes, w_ref, *refs):
    ins, refs = refs[: len(given)], refs[len(given) :]
    acc_ref = refs[-1]
    layers = w_ref.shape[0]
    refs = refs[resumes:]
    where = dict(zip(given, ins, strict=True))
    kept_at = dict(zip(kept, refs[: len(kept)], strict=True))
    held = {key: halves(ref[...]) for key, ref in where.items()}
    for n, (layer, place) in enumerate(work):
        total = conv_plane(w_ref[layer - 1], [held[layer - 1, place + d] for d in (-1, 0, 1)], acc_ref.at[n % 2])
        if layer == layers:
            store_cells(refs[len(kept)], place - first, where[0, place][...] + total)
            continue
        total = gelu(total)
        held[layer, place] = halves(total)
        if (layer, place) in kept_at:
            kept_at[layer, place][...] = total


def mlp_kernel(y_ref, a_ref, b_ref, out_ref, hh_ref, hl_ref):
    channels = y_ref.shape[0]
    hidden = hh_ref.shape[0]
    rows = 256
    y = y_ref[...]
    scale = lax.rsqrt(jnp.mean(y * y, axis=0, keepdims=True) + 1e-06)
    hi, lo = halves(y * scale)
    seen = jnp.concatenate([hi, lo, hi], axis=0)
    for r in range(0, hidden, rows):
        top, low = a_ref[r : r + rows, :], a_ref[hidden + r : hidden + r + rows, :]
        hid = gelu(jnp.dot(jnp.concatenate([top, top, low], axis=1), seen, preferred_element_type=F32))
        hh, hl = halves(hid)
        hh_ref[r : r + rows, :] = hh
        hl_ref[r : r + rows, :] = hl
    seen = jnp.concatenate([hh_ref[...], hl_ref[...], hh_ref[...]], axis=0)
    for r in range(0, channels, rows):
        top, low = b_ref[r : r + rows, :], b_ref[channels + r : channels + r + rows, :]
        part = jnp.concatenate([top, top, low], axis=1)
        out_ref[r : r + rows, :] = y_ref[r : r + rows, :] + jnp.dot(part, seen, preferred_element_type=F32)


def place_kernel(in_ref, out_ref):
    size = in_ref.shape[2]
    runs = out_ref.shape[2] // size
    last = out_ref.shape[1] - 1
    flip = turned_here()
    for p in range(last + 1):
        for q in range(runs):
            out_ref[:, p, q * size : (q + 1) * size] = jnp.where(
                flip, in_ref[(last - p) * runs + q], in_ref[p * runs + q]
            )

def per_device(volume, conv_weight, norm_gain, mlp_in, mlp_out):
    width, planes, cells = volume.shape
    count = lax.axis_size("depth")
    members = lax.axis_size("chan")
    kernels = conv_weight[0, :, 0]
    layers = kernels.shape[0]
    channels, hidden = mlp_out.shape[1], mlp_out.shape[2]
    size = planes * cells // members
    plane = jax.ShapeDtypeStruct((width, cells), F32)

    pair = [(i, i ^ 1) for i in range(count)]
    along = [(i, (i + (2 if i % 2 == 0 else count - 2)) % count) for i in range(count)]
    own = call(planes_kernel, (plane,) * planes, 0, volume.size * 8, [VMEM])(volume)
    there = [lax.ppermute(q, "depth", pair) for q in own[:2]]
    taps = call(
        taps_kernel,
        jax.ShapeDtypeStruct((layers, 9 * width, 384), BF16),
        0,
        kernels.size * 8,
        [VMEM],
        [pltpu.VMEM((width, 1024), F32)],
    )(kernels)
    held = {(0, 3 + k): v for k, v in enumerate(own)}

    def stage(given, work, kept, finished=None):
        outs = (plane,) * len(kept)
        if any(layer == layers for layer, _ in work):
            outs += (jax.ShapeDtypeStruct((members, width, size), F32),)
        more = [] if finished is None else [finished]
        got = call(
            functools.partial(stage_kernel, given, work, kept, layers, len(more)),
            outs,
            len(work) * 2 * 288 * 384 * cells,
            (len(given) + len(outs)) * width * cells * 4,
            [VMEM] * (1 + len(given) + len(more)),
            [pltpu.VMEM((2, 9 * width, cells), F32)],
            {1 + len(given): len(kept)} if more else None,
        )(taps, *[held[key] for key in given], *more)
        held.update(zip(kept, got))
        return got[-1]

    stage(((0, 3), (0, 4), (0, 5), (0, 6)), ((1, 4), (1, 5)), ((1, 4), (1, 5)))
    weights = jax.ShapeDtypeStruct((2 * hidden, channels), BF16)
    w_in = call(first_weights_kernel, weights, 0, mlp_in.size * 8, [VMEM] * 2)(norm_gain, mlp_in[0])
    third, held[1, 4], held[1, 5] = lax.optimization_barrier((own[2], held[1, 4], held[1, 5]))
    weights = jax.ShapeDtypeStruct((2 * channels, hidden), BF16)
    w_out = call(second_weights_kernel, weights, 0, mlp_out.size * 8, [VMEM])(mlp_out[0])
    fourth, w_out = lax.optimization_barrier((own[3], w_out))
    there[1], w_in = lax.optimization_barrier((there[1], w_in))
    there += [lax.ppermute(q, "depth", pair) for q in (third, fourth)]
    for k in range(layers):
        held[0, 2 - k] = lax.ppermute(there[k], "depth", along)
        held[0, 9 - k] = there[k + 1]
    stage(((0, 2), (0, 3), (0, 4), (1, 4), (1, 5)), ((1, 3), (2, 4)), ((1, 3), (2, 4)))
    stage(((0, 1), (0, 2), (0, 3), (1, 3), (1, 4)), ((1, 2), (2, 3)), ((1, 2), (2, 3)))
    most = stage(
        ((0, 4), (0, 5), (0, 6), (0, 7), (0, 8), (0, 9), (1, 4), (1, 5), (2, 3), (2, 4)),
        ((1, 6), (1, 7), (1, 8), (2, 5), (2, 6), (2, 7), (3, 4), (3, 5), (3, 6)),
        (),
    )
    mixed = stage(
        ((0, 0), (0, 1), (0, 2), (0, 3), (1, 2), (1, 3), (2, 3), (2, 4)), ((1, 1), (2, 2), (3, 3)), (), most
    )
    here = lax.all_to_all(mixed, "chan", split_axis=0, concat_axis=0, tiled=True)
    out = call(
        mlp_kernel,
        jax.ShapeDtypeStruct((channels, size), F32),
        12 * hidden * channels * size,
        mlp_in.size * 8,
        [VMEM] * 3,
        [pltpu.VMEM((hidden, size), BF16)] * 2,
    )(here.reshape(channels, size), w_in, w_out)
    back = lax.all_to_all(out.reshape(members, width, size), "chan", split_axis=0, concat_axis=0, tiled=True)
    return call(place_kernel, jax.ShapeDtypeStruct(volume.shape, F32), 0, volume.size * 8, [VMEM])(back)


def solution(mesh):
    in_specs = (P("chan", "depth", None), P(None, None, "chan", None, None), P(), P(), P())
    out_specs = P("chan", "depth", None)
    return jax.shard_map(
        per_device, mesh=mesh, in_specs=in_specs, out_specs=out_specs, check_vma=False
    )
```

```python
import functools

import jax
import jax.numpy as jnp
from jax import lax
from jax.experimental import pallas as pl
from jax.experimental.pallas import tpu as pltpu
from jax.sharding import PartitionSpec as P

W = 32
F32 = jnp.float32
BF16 = jnp.bfloat16
VMEM = pl.BlockSpec(memory_space=pltpu.VMEM)


def call(body, outs, flops, moved, ins, scratch=(), aliases=None):
    return pl.pallas_call(
        body,
        out_shape=outs,
        in_specs=ins,
        out_specs=jax.tree.map(lambda _: VMEM, outs),
        scratch_shapes=scratch,
        input_output_aliases=aliases or {},
        cost_estimate=pl.CostEstimate(flops=flops, bytes_accessed=moved, transcendentals=0),
        compiler_params=pltpu.CompilerParams(vmem_limit_bytes=32 << 20),
    )


def halves(x):
    hi = x.astype(BF16)
    return hi, (x - hi.astype(F32)).astype(BF16)


def gelu(v):
    return 0.5 * v * (1.0 + jnp.tanh(0.7978845608028654 * (v + 0.044715 * (v * v * v))))


def turned_here():
    return lax.axis_index("depth") % 2 > 0


def rearranged(pieces, back):
    block = lax.broadcasted_iota(jnp.int32, pieces[0].shape, 1) // W
    count = len(pieces)
    runs = 128 // W
    moved = []
    for v in range(count):
        total = None
        for b in range(runs):
            if back:
                row = v * runs + b
                source, at = row % count, row // count
            else:
                row = b * count + v
                source, at = row // runs, row % runs
            piece = pieces[source]
            if at != b:
                piece = pltpu.roll(piece, (b - at) * W % 128, 1)
            total = piece if total is None else jnp.where(block == b, piece, total)
        moved.append(total)
    return moved


def planes_kernel(places, x_ref, *q_refs):
    last = x_ref.shape[1] - 1
    flip = turned_here()
    for k, q_ref in zip(places, q_refs, strict=True):
        plane = jnp.where(flip, x_ref[:, last - k, :], x_ref[:, k, :])
        pieces = [plane[:, v : v + 128] for v in range(0, plane.shape[1], 128)]
        q_ref[...] = jnp.concatenate(rearranged(pieces, False), axis=1)


def taps_kernel(k_ref, w_ref, pad_ref):
    layers, width, taps = k_ref.shape
    flip = turned_here()
    lane = lax.broadcasted_iota(jnp.int32, (width, 128), 1)
    pad_ref[...] = jnp.zeros_like(pad_ref)
    for layer in range(layers):
        pad_ref[:, :taps] = k_ref[layer]
        for tap in range(9):
            start = tap * 3 * width
            base, shift = start // 128 * 128, start % 128
            pair = pad_ref[:, base : base + 256]
            if shift:
                pair = pltpu.roll(pair, 256 - shift, 1)
            ahead = pair[:, :128]
            turned = jnp.where(lane // width == 1, ahead, pltpu.roll(ahead, 2 * width, 1))
            hi, lo = halves(jnp.where(lane < 3 * width, jnp.where(flip, turned, ahead), 0.0))
            rows = pl.ds(tap * width, width)
            w_ref[layer, rows, 0:128] = hi
            w_ref[layer, rows, 128:256] = hi
            w_ref[layer, rows, 256:384] = lo


def first_weights_kernel(gain_ref, a_ref, w_ref):
    gain = gain_ref[...]
    hidden = a_ref.shape[0]
    rows = 128
    for r in range(0, hidden, rows):
        hi, lo = halves(a_ref[r : r + rows, :] * gain)
        w_ref[r : r + rows, :] = hi
        w_ref[hidden + r : hidden + r + rows, :] = lo


def second_weights_kernel(b_ref, w_ref):
    channels = b_ref.shape[0]
    rows = 128
    for r in range(0, channels, rows):
        hi, lo = halves(b_ref[r : r + rows, :])
        w_ref[r : r + rows, :] = hi
        w_ref[channels + r : channels + r + rows, :] = lo


def conv_plane(weight, three, acc_ref):
    zero = jnp.zeros_like(three[0][0])
    his = [t[0] for t in three] + [zero]
    los = [t[1] for t in three] + [zero]
    acc_ref[...] = jnp.dot(weight, jnp.concatenate(his + los + his, axis=0), preferred_element_type=F32)
    width, cells = zero.shape
    count = cells // 128

    def tap(b, c, v):
        return acc_ref[(b * 3 + c) * width : (b * 3 + c + 1) * width, v * 128 : (v + 1) * 128]

    def rows(c, v):
        above = tap(0, c, v - 1) if v else pltpu.roll(tap(0, c, count - 1), W, 1)
        below = tap(2, c, v + 1) if v < count - 1 else pltpu.roll(tap(2, c, 0), 128 - W, 1)
        return tap(1, c, v) + above + below

    column = lax.broadcasted_iota(jnp.int32, (width, 128), 1) % W
    parts = []
    for v in range(count):
        left, here, right = (rows(c, v) for c in range(3))
        left = jnp.where(column == 0, pltpu.roll(left, 128 - W + 1, 1), pltpu.roll(left, 1, 1))
        right = jnp.where(column == W - 1, pltpu.roll(right, W - 1, 1), pltpu.roll(right, 127, 1))
        parts.append(left + here + right)
    return jnp.concatenate(parts, axis=1)


def store_cells(out_ref, plane, value):
    size = out_ref.shape[2]
    runs = value.shape[1] // size
    for q in range(runs):
        out_ref[plane * runs + q] = value[:, q * size : (q + 1) * size]


def stage_kernel(given, work, kept, first, resumes, w_ref, *refs):
    ins, refs = refs[: len(given)], refs[len(given) :]
    acc_ref = refs[-1]
    layers = w_ref.shape[0]
    refs = refs[resumes:]
    where = dict(zip(given, ins, strict=True))
    kept_at = dict(zip(kept, refs[: len(kept)], strict=True))
    held = {key: halves(ref[...]) for key, ref in where.items()}
    for n, (layer, place) in enumerate(work):
        total = conv_plane(w_ref[layer - 1], [held[layer - 1, place + d] for d in (-1, 0, 1)], acc_ref.at[n % 2])
        if layer == layers:
            store_cells(refs[len(kept)], place - first, where[0, place][...] + total)
            continue
        total = gelu(total)
        held[layer, place] = halves(total)
        if (layer, place) in kept_at:
            kept_at[layer, place][...] = total


def mlp_kernel(y_ref, a_ref, b_ref, out_ref, hh_ref, hl_ref):
    channels = y_ref.shape[0]
    hidden = hh_ref.shape[0]
    rows = 256
    y = y_ref[...]
    scale = lax.rsqrt(jnp.mean(y * y, axis=0, keepdims=True) + 1e-06)
    hi, lo = halves(y * scale)
    seen = jnp.concatenate([hi, lo, hi], axis=0)
    for r in range(0, hidden, rows):
        top, low = a_ref[r : r + rows, :], a_ref[hidden + r : hidden + r + rows, :]
        hid = gelu(jnp.dot(jnp.concatenate([top, top, low], axis=1), seen, preferred_element_type=F32))
        hh, hl = halves(hid)
        hh_ref[r : r + rows, :] = hh
        hl_ref[r : r + rows, :] = hl
    seen = jnp.concatenate([hh_ref[...], hl_ref[...], hh_ref[...]], axis=0)
    for r in range(0, channels, rows):
        top, low = b_ref[r : r + rows, :], b_ref[channels + r : channels + r + rows, :]
        part = jnp.concatenate([top, top, low], axis=1)
        out_ref[r : r + rows, :] = y_ref[r : r + rows, :] + jnp.dot(part, seen, preferred_element_type=F32)


def place_kernel(in_ref, out_ref):
    size = in_ref.shape[2]
    runs = out_ref.shape[2] // size
    last = out_ref.shape[1] - 1
    flip = turned_here()
    for p in range(last + 1):
        start = jnp.where(flip, last - p, p) * runs
        pieces = [in_ref[start + q, :, v : v + 128] for q in range(runs) for v in range(0, size, 128)]
        for v, piece in enumerate(rearranged(pieces, True)):
            out_ref[:, p, v * 128 : (v + 1) * 128] = piece


def per_device(volume, conv_weight, norm_gain, mlp_in, mlp_out):
    width, planes, cells = volume.shape
    count = lax.axis_size("depth")
    members = lax.axis_size("chan")
    kernels = conv_weight[0, :, 0]
    layers = kernels.shape[0]
    channels, hidden = mlp_out.shape[1], mlp_out.shape[2]
    size = planes * cells // members
    plane = jax.ShapeDtypeStruct((width, cells), F32)

    pair = [(i, i ^ 1) for i in range(count)]
    along = [(i, (i + (2 if i % 2 == 0 else count - 2)) % count) for i in range(count)]
    own = []
    for places in ((0,), tuple(range(1, planes))):
        body = functools.partial(planes_kernel, places)
        own += call(body, (plane,) * len(places), 0, len(places) * width * cells * 8, [VMEM])(volume)
    there = [lax.ppermute(q, "depth", pair) for q in own[:2]]
    taps = call(
        taps_kernel,
        jax.ShapeDtypeStruct((layers, 9 * width, 384), BF16),
        0,
        kernels.size * 8,
        [VMEM],
        [pltpu.VMEM((width, 1024), F32)],
    )(kernels)
    held = {(0, 3 + k): v for k, v in enumerate(own)}

    def stage(given, work, kept, finished=None):
        outs = (plane,) * len(kept)
        if any(layer == layers for layer, _ in work):
            outs += (jax.ShapeDtypeStruct((members, width, size), F32),)
        more = [] if finished is None else [finished]
        got = call(
            functools.partial(stage_kernel, given, work, kept, layers, len(more)),
            outs,
            len(work) * 2 * 288 * 384 * cells,
            (len(given) + len(outs)) * width * cells * 4,
            [VMEM] * (1 + len(given) + len(more)),
            [pltpu.VMEM((2, 9 * width, cells), F32)],
            {1 + len(given): len(kept)} if more else None,
        )(taps, *[held[key] for key in given], *more)
        held.update(zip(kept, got))
        return got[-1]

    stage(((0, 3), (0, 4), (0, 5), (0, 6)), ((1, 4), (1, 5)), ((1, 4), (1, 5)))
    weights = jax.ShapeDtypeStruct((2 * hidden, channels), BF16)
    w_in = call(first_weights_kernel, weights, 0, mlp_in.size * 8, [VMEM] * 2)(norm_gain, mlp_in[0])
    third, held[1, 4], held[1, 5] = lax.optimization_barrier((own[2], held[1, 4], held[1, 5]))
    weights = jax.ShapeDtypeStruct((2 * channels, hidden), BF16)
    w_out = call(second_weights_kernel, weights, 0, mlp_out.size * 8, [VMEM])(mlp_out[0])
    fourth, w_out = lax.optimization_barrier((own[3], w_out))
    there[1], w_in = lax.optimization_barrier((there[1], w_in))
    there += [lax.ppermute(q, "depth", pair) for q in (third, fourth)]
    for k in range(layers):
        held[0, 2 - k] = lax.ppermute(there[k], "depth", along)
        held[0, 9 - k] = there[k + 1]
    stage(((0, 2), (0, 3), (0, 4), (1, 4), (1, 5)), ((1, 3), (2, 4)), ((1, 3), (2, 4)))
    most = stage(
        ((0, 5), (0, 6), (0, 7), (0, 8), (0, 9), (1, 4), (1, 5), (2, 4)),
        ((1, 6), (1, 7), (1, 8), (2, 5), (2, 6), (2, 7), (3, 5), (3, 6)),
        ((2, 5),),
    )
    mixed = stage(
        ((0, 0), (0, 1), (0, 2), (0, 3), (0, 4), (1, 3), (1, 4), (2, 4), (2, 5)),
        ((1, 2), (1, 1), (2, 3), (2, 2), (3, 4), (3, 3)),
        (),
        most,
    )
    here = lax.all_to_all(mixed, "chan", split_axis=0, concat_axis=0, tiled=True)
    out = call(
        mlp_kernel,
        jax.ShapeDtypeStruct((channels, size), F32),
        12 * hidden * channels * size,
        mlp_in.size * 8,
        [VMEM] * 3,
        [pltpu.VMEM((hidden, size), BF16)] * 2,
    )(here.reshape(channels, size), w_in, w_out)
    back = lax.all_to_all(out.reshape(members, width, size), "chan", split_axis=0, concat_axis=0, tiled=True)
    return call(place_kernel, jax.ShapeDtypeStruct(volume.shape, F32), 0, volume.size * 8, [VMEM])(back)


def solution(mesh):
    in_specs = (P("chan", "depth", None), P(None, None, "chan", None, None), P(), P(), P())
    out_specs = P("chan", "depth", None)
    return jax.shard_map(
        per_device, mesh=mesh, in_specs=in_specs, out_specs=out_specs, check_vma=False
    )
```

```python
import functools

import jax
import jax.numpy as jnp
from jax import lax
from jax.experimental import pallas as pl
from jax.experimental.pallas import tpu as pltpu
from jax.sharding import PartitionSpec as P

W = 32
PARTS = 4
F32 = jnp.float32
BF16 = jnp.bfloat16
VMEM = pl.BlockSpec(memory_space=pltpu.VMEM)
HBM = pl.BlockSpec(memory_space=pltpu.HBM)


def call(body, outs, flops, moved, ins, scratch=(), aliases=None, outs_in=VMEM):
    return pl.pallas_call(
        body,
        out_shape=outs,
        in_specs=ins,
        out_specs=jax.tree.map(lambda _: outs_in, outs),
        scratch_shapes=scratch,
        input_output_aliases=aliases or {},
        cost_estimate=pl.CostEstimate(flops=flops, bytes_accessed=moved, transcendentals=0),
        compiler_params=pltpu.CompilerParams(vmem_limit_bytes=32 << 20),
    )


def halves(x):
    hi = x.astype(BF16)
    return hi, (x - hi.astype(F32)).astype(BF16)


def gelu(v):
    return 0.5 * v * (1.0 + jnp.tanh(0.7978845608028654 * (v + 0.044715 * (v * v * v))))


def turned_here():
    return lax.axis_index("depth") % 2 > 0


def rearranged(pieces, back):
    block = lax.broadcasted_iota(jnp.int32, pieces[0].shape, 1) // W
    count = len(pieces)
    runs = 128 // W
    moved = []
    for v in range(count):
        total = None
        for b in range(runs):
            if back:
                row = v * runs + b
                source, at = row % count, row // count
            else:
                row = b * count + v
                source, at = row // runs, row % runs
            piece = pieces[source]
            if at != b:
                piece = pltpu.roll(piece, (b - at) * W % 128, 1)
            total = piece if total is None else jnp.where(block == b, piece, total)
        moved.append(total)
    return moved


def planes_kernel(places, x_ref, *q_refs):
    last = x_ref.shape[1] - 1
    flip = turned_here()
    for k, q_ref in zip(places, q_refs, strict=True):
        plane = jnp.where(flip, x_ref[:, last - k, :], x_ref[:, k, :])
        pieces = [plane[:, v : v + 128] for v in range(0, plane.shape[1], 128)]
        q_ref[...] = jnp.concatenate(rearranged(pieces, False), axis=1)


def taps_kernel(k_ref, w_ref, pad_ref):
    layers, width, taps = k_ref.shape
    flip = turned_here()
    lane = lax.broadcasted_iota(jnp.int32, (width, 128), 1)
    pad_ref[...] = jnp.zeros_like(pad_ref)
    for layer in range(layers):
        pad_ref[:, :taps] = k_ref[layer]
        for tap in range(9):
            start = tap * 3 * width
            base, shift = start // 128 * 128, start % 128
            pair = pad_ref[:, base : base + 256]
            if shift:
                pair = pltpu.roll(pair, 256 - shift, 1)
            ahead = pair[:, :128]
            turned = jnp.where(lane // width == 1, ahead, pltpu.roll(ahead, 2 * width, 1))
            hi, lo = halves(jnp.where(lane < 3 * width, jnp.where(flip, turned, ahead), 0.0))
            rows = pl.ds(tap * width, width)
            w_ref[layer, rows, 0:128] = hi
            w_ref[layer, rows, 128:256] = hi
            w_ref[layer, rows, 256:384] = lo


def first_weights_kernel(gain_ref, a_ref, w_ref):
    gain = gain_ref[...]
    hidden = a_ref.shape[0]
    rows = 128
    for r in range(0, hidden, rows):
        hi, lo = halves(a_ref[r : r + rows, :] * gain)
        w_ref[r : r + rows, :] = hi
        w_ref[hidden + r : hidden + r + rows, :] = lo


def second_weights_kernel(b_ref, w_ref):
    channels = b_ref.shape[0]
    rows = 128
    for r in range(0, channels, rows):
        hi, lo = halves(b_ref[r : r + rows, :])
        w_ref[r : r + rows, :] = hi
        w_ref[channels + r : channels + r + rows, :] = lo


def conv_plane(weight, three, acc_ref):
    zero = jnp.zeros_like(three[0][0])
    his = [t[0] for t in three] + [zero]
    los = [t[1] for t in three] + [zero]
    acc_ref[...] = jnp.dot(weight, jnp.concatenate(his + los + his, axis=0), preferred_element_type=F32)
    width, cells = zero.shape
    count = cells // 128

    def tap(b, c, v):
        return acc_ref[(b * 3 + c) * width : (b * 3 + c + 1) * width, v * 128 : (v + 1) * 128]

    def rows(c, v):
        above = tap(0, c, v - 1) if v else pltpu.roll(tap(0, c, count - 1), W, 1)
        below = tap(2, c, v + 1) if v < count - 1 else pltpu.roll(tap(2, c, 0), 128 - W, 1)
        return tap(1, c, v) + above + below

    column = lax.broadcasted_iota(jnp.int32, (width, 128), 1) % W
    parts = []
    for v in range(count):
        left, here, right = (rows(c, v) for c in range(3))
        left = jnp.where(column == 0, pltpu.roll(left, 128 - W + 1, 1), pltpu.roll(left, 1, 1))
        right = jnp.where(column == W - 1, pltpu.roll(right, W - 1, 1), pltpu.roll(right, 127, 1))
        parts.append(left + here + right)
    return jnp.concatenate(parts, axis=1)


def store_cells(out_ref, plane, value):
    size = out_ref.shape[2]
    runs = value.shape[1] // size
    for q in range(runs):
        out_ref[plane * runs + q] = value[:, q * size : (q + 1) * size]


def stage_kernel(given, work, kept, first, resumes, w_ref, *refs):
    ins, refs = refs[: len(given)], refs[len(given) :]
    acc_ref = refs[-1]
    layers = w_ref.shape[0]
    refs = refs[resumes:]
    where = dict(zip(given, ins, strict=True))
    kept_at = dict(zip(kept, refs[: len(kept)], strict=True))
    held = {key: halves(ref[...]) for key, ref in where.items()}
    for n, (layer, place) in enumerate(work):
        total = conv_plane(w_ref[layer - 1], [held[layer - 1, place + d] for d in (-1, 0, 1)], acc_ref.at[n % 2])
        if layer == layers:
            store_cells(refs[len(kept)], place - first, where[0, place][...] + total)
            continue
        total = gelu(total)
        held[layer, place] = halves(total)
        if (layer, place) in kept_at:
            kept_at[layer, place][...] = total


def mlp_kernel(y_ref, a_ref, b_ref, out_ref, hh_ref, hl_ref):
    channels = y_ref.shape[0]
    hidden = hh_ref.shape[0]
    rows = 256
    y = y_ref[...]
    scale = lax.rsqrt(jnp.mean(y * y, axis=0, keepdims=True) + 1e-06)
    hi, lo = halves(y * scale)
    seen = jnp.concatenate([hi, lo, hi], axis=0)
    for r in range(0, hidden, rows):
        top, low = a_ref[r : r + rows, :], a_ref[hidden + r : hidden + r + rows, :]
        hid = gelu(jnp.dot(jnp.concatenate([top, top, low], axis=1), seen, preferred_element_type=F32))
        hh, hl = halves(hid)
        hh_ref[r : r + rows, :] = hh
        hl_ref[r : r + rows, :] = hl
    seen = jnp.concatenate([hh_ref[...], hl_ref[...], hh_ref[...]], axis=0)
    for r in range(0, channels, rows):
        top, low = b_ref[r : r + rows, :], b_ref[channels + r : channels + r + rows, :]
        part = jnp.concatenate([top, top, low], axis=1)
        out_ref[r : r + rows, :] = y_ref[r : r + rows, :] + jnp.dot(part, seen, preferred_element_type=F32)


def place_kernel(in_ref, out_hbm, held_ref, sems):
    size = in_ref.shape[2]
    width, planes, cells = out_hbm.shape
    runs = cells // size
    flip = turned_here()
    rows = width // sems.shape[0]
    copies = []
    for n in range(width // rows):
        part = slice(n * rows, (n + 1) * rows)
        for p in range(planes):
            start = jnp.where(flip, planes - 1 - p, p) * runs
            pieces = [in_ref[start + q, part, v : v + 128] for q in range(runs) for v in range(0, size, 128)]
            for v, piece in enumerate(rearranged(pieces, True)):
                held_ref[part, p, v * 128 : (v + 1) * 128] = piece
        part = pl.ds(n * rows, rows)
        copies.append(pltpu.make_async_copy(held_ref.at[part], out_hbm.at[part], sems.at[n]))
        copies[-1].start()
    for copy in copies:
        copy.wait()


def per_device(volume, conv_weight, norm_gain, mlp_in, mlp_out):
    width, planes, cells = volume.shape
    count = lax.axis_size("depth")
    members = lax.axis_size("chan")
    kernels = conv_weight[0, :, 0]
    layers = kernels.shape[0]
    channels, hidden = mlp_out.shape[1], mlp_out.shape[2]
    size = planes * cells // members
    plane = jax.ShapeDtypeStruct((width, cells), F32)

    pair = [(i, i ^ 1) for i in range(count)]
    along = [(i, (i + (2 if i % 2 == 0 else count - 2)) % count) for i in range(count)]
    own = []
    for places in ((0,), tuple(range(1, planes))):
        body = functools.partial(planes_kernel, places)
        own += call(body, (plane,) * len(places), 10**9, len(places) * width * cells * 8, [VMEM])(volume)
    there = [lax.ppermute(q, "depth", pair) for q in own[:2]]
    taps = call(
        taps_kernel,
        jax.ShapeDtypeStruct((layers, 9 * width, 384), BF16),
        0,
        kernels.size * 8,
        [VMEM],
        [pltpu.VMEM((width, 1024), F32)],
    )(kernels)
    held = {(0, 3 + k): v for k, v in enumerate(own)}

    def stage(given, work, kept, finished=None):
        outs = (plane,) * len(kept)
        if any(layer == layers for layer, _ in work):
            outs += (jax.ShapeDtypeStruct((members, width, size), F32),)
        more = [] if finished is None else [finished]
        got = call(
            functools.partial(stage_kernel, given, work, kept, layers, len(more)),
            outs,
            len(work) * 2 * 288 * 384 * cells,
            (len(given) + len(outs)) * width * cells * 4,
            [VMEM] * (1 + len(given) + len(more)),
            [pltpu.VMEM((2, 9 * width, cells), F32)],
            {1 + len(given): len(kept)} if more else None,
        )(taps, *[held[key] for key in given], *more)
        held.update(zip(kept, got))
        return got[-1]

    stage(((0, 3), (0, 4), (0, 5), (0, 6)), ((1, 4), (1, 5)), ((1, 4), (1, 5)))
    weights = jax.ShapeDtypeStruct((2 * hidden, channels), BF16)
    w_in = call(first_weights_kernel, weights, 0, mlp_in.size * 8, [VMEM] * 2)(norm_gain, mlp_in[0])
    third, held[1, 4], held[1, 5] = lax.optimization_barrier((own[2], held[1, 4], held[1, 5]))
    weights = jax.ShapeDtypeStruct((2 * channels, hidden), BF16)
    w_out = call(second_weights_kernel, weights, 0, mlp_out.size * 8, [VMEM])(mlp_out[0])
    fourth, w_out = lax.optimization_barrier((own[3], w_out))
    there[1], w_in = lax.optimization_barrier((there[1], w_in))
    there += [lax.ppermute(q, "depth", pair) for q in (third, fourth)]
    for k in range(layers):
        held[0, 2 - k] = lax.ppermute(there[k], "depth", along)
        held[0, 9 - k] = there[k + 1]
    stage(((0, 2), (0, 3), (0, 4), (1, 4), (1, 5)), ((1, 3), (2, 4)), ((1, 3), (2, 4)))
    most = stage(
        ((0, 5), (0, 6), (0, 7), (0, 8), (0, 9), (1, 4), (1, 5), (2, 4)),
        ((1, 6), (1, 7), (1, 8), (2, 5), (2, 6), (2, 7), (3, 5), (3, 6)),
        ((2, 5),),
    )
    mixed = stage(
        ((0, 0), (0, 1), (0, 2), (0, 3), (0, 4), (1, 3), (1, 4), (2, 4), (2, 5)),
        ((1, 2), (1, 1), (2, 3), (2, 2), (3, 4), (3, 3)),
        (),
        most,
    )
    here = lax.all_to_all(mixed, "chan", split_axis=0, concat_axis=0, tiled=True)
    out = call(
        mlp_kernel,
        jax.ShapeDtypeStruct((channels, size), F32),
        12 * hidden * channels * size,
        mlp_in.size * 8,
        [VMEM] * 3,
        [pltpu.VMEM((hidden, size), BF16)] * 2,
    )(here.reshape(channels, size), w_in, w_out)
    back = lax.all_to_all(out.reshape(members, width, size), "chan", split_axis=0, concat_axis=0, tiled=True)
    return call(
        place_kernel,
        jax.ShapeDtypeStruct(volume.shape, F32),
        0,
        volume.size * 8,
        [VMEM],
        [pltpu.VMEM(volume.shape, F32), pltpu.SemaphoreType.DMA((PARTS,))],
        outs_in=HBM,
    )(back)


def solution(mesh):
    in_specs = (P("chan", "depth", None), P(None, None, "chan", None, None), P(), P(), P())
    out_specs = P("chan", "depth", None)
    return jax.shard_map(
        per_device, mesh=mesh, in_specs=in_specs, out_specs=out_specs, check_vma=False
    )
```

```python
import functools

import jax
import jax.numpy as jnp
from jax import lax
from jax.experimental import pallas as pl
from jax.experimental.pallas import tpu as pltpu
from jax.sharding import PartitionSpec as P

W = 32
PARTS = 4
F32 = jnp.float32
BF16 = jnp.bfloat16
VMEM = pl.BlockSpec(memory_space=pltpu.VMEM)
HBM = pl.BlockSpec(memory_space=pltpu.HBM)


def call(body, outs, flops, moved, ins, scratch=(), aliases=None, outs_in=VMEM):
    return pl.pallas_call(
        body,
        out_shape=outs,
        in_specs=ins,
        out_specs=jax.tree.map(lambda _: outs_in, outs),
        scratch_shapes=scratch,
        input_output_aliases=aliases or {},
        cost_estimate=pl.CostEstimate(flops=flops, bytes_accessed=moved, transcendentals=0),
        compiler_params=pltpu.CompilerParams(vmem_limit_bytes=32 << 20),
    )


def halves(x):
    hi = x.astype(BF16)
    return hi, (x - hi.astype(F32)).astype(BF16)


def gelu(v):
    return 0.5 * v * (1.0 + jnp.tanh(0.7978845608028654 * (v + 0.044715 * (v * v * v))))


def turned_here():
    return lax.axis_index("depth") % 2 > 0


def rearranged(pieces, back):
    block = lax.broadcasted_iota(jnp.int32, pieces[0].shape, 1) // W
    count = len(pieces)
    runs = 128 // W
    moved = []
    for v in range(count):
        total = None
        for b in range(runs):
            if back:
                row = v * runs + b
                source, at = row % count, row // count
            else:
                row = b * count + v
                source, at = row // runs, row % runs
            piece = pieces[source]
            if at != b:
                piece = pltpu.roll(piece, (b - at) * W % 128, 1)
            total = piece if total is None else jnp.where(block == b, piece, total)
        moved.append(total)
    return moved


def planes_kernel(places, x_hbm, *refs):
    q_refs, (held_ref, sems) = refs[:-2], refs[-2:]
    last = x_hbm.shape[1] - 1
    flip = turned_here()
    copies = []
    for n, k in enumerate(places):
        place = jnp.where(flip, last - k, k)
        copies.append(pltpu.make_async_copy(x_hbm.at[:, place, :], held_ref.at[n], sems.at[n]))
        copies[-1].start()
    for n, q_ref in enumerate(q_refs):
        copies[n].wait()
        pieces = [held_ref[n, :, v : v + 128] for v in range(0, q_ref.shape[1], 128)]
        q_ref[...] = jnp.concatenate(rearranged(pieces, False), axis=1)


def taps_kernel(k_ref, w_ref, pad_ref):
    layers, width, taps = k_ref.shape
    flip = turned_here()
    lane = lax.broadcasted_iota(jnp.int32, (width, 128), 1)
    pad_ref[...] = jnp.zeros_like(pad_ref)
    for layer in range(layers):
        pad_ref[:, :taps] = k_ref[layer]
        for tap in range(9):
            start = tap * 3 * width
            base, shift = start // 128 * 128, start % 128
            pair = pad_ref[:, base : base + 256]
            if shift:
                pair = pltpu.roll(pair, 256 - shift, 1)
            ahead = pair[:, :128]
            turned = jnp.where(lane // width == 1, ahead, pltpu.roll(ahead, 2 * width, 1))
            hi, lo = halves(jnp.where(lane < 3 * width, jnp.where(flip, turned, ahead), 0.0))
            rows = pl.ds(tap * width, width)
            w_ref[layer, rows, 0:128] = hi
            w_ref[layer, rows, 128:256] = hi
            w_ref[layer, rows, 256:384] = lo


def first_weights_kernel(gain_ref, a_ref, w_ref):
    gain = gain_ref[...]
    hidden = a_ref.shape[0]
    rows = 128
    for r in range(0, hidden, rows):
        hi, lo = halves(a_ref[r : r + rows, :] * gain)
        w_ref[r : r + rows, :] = hi
        w_ref[hidden + r : hidden + r + rows, :] = lo


def second_weights_kernel(b_ref, w_ref):
    channels = b_ref.shape[0]
    rows = 128
    for r in range(0, channels, rows):
        hi, lo = halves(b_ref[r : r + rows, :])
        w_ref[r : r + rows, :] = hi
        w_ref[channels + r : channels + r + rows, :] = lo


def conv_plane(weight, three, acc_ref):
    zero = jnp.zeros_like(three[0][0])
    his = [t[0] for t in three] + [zero]
    los = [t[1] for t in three] + [zero]
    acc_ref[...] = jnp.dot(weight, jnp.concatenate(his + los + his, axis=0), preferred_element_type=F32)
    width, cells = zero.shape
    count = cells // 128

    def tap(b, c, v):
        return acc_ref[(b * 3 + c) * width : (b * 3 + c + 1) * width, v * 128 : (v + 1) * 128]

    def rows(c, v):
        above = tap(0, c, v - 1) if v else pltpu.roll(tap(0, c, count - 1), W, 1)
        below = tap(2, c, v + 1) if v < count - 1 else pltpu.roll(tap(2, c, 0), 128 - W, 1)
        return tap(1, c, v) + above + below

    column = lax.broadcasted_iota(jnp.int32, (width, 128), 1) % W
    parts = []
    for v in range(count):
        left, here, right = (rows(c, v) for c in range(3))
        left = jnp.where(column == 0, pltpu.roll(left, 128 - W + 1, 1), pltpu.roll(left, 1, 1))
        right = jnp.where(column == W - 1, pltpu.roll(right, W - 1, 1), pltpu.roll(right, 127, 1))
        parts.append(left + here + right)
    return jnp.concatenate(parts, axis=1)


def store_cells(out_ref, plane, value):
    size = out_ref.shape[2]
    runs = value.shape[1] // size
    for q in range(runs):
        out_ref[plane * runs + q] = value[:, q * size : (q + 1) * size]


def stage_kernel(given, work, kept, first, resumes, w_ref, *refs):
    ins, refs = refs[: len(given)], refs[len(given) :]
    acc_ref = refs[-1]
    layers = w_ref.shape[0]
    refs = refs[resumes:]
    where = dict(zip(given, ins, strict=True))
    kept_at = dict(zip(kept, refs[: len(kept)], strict=True))
    held = {key: halves(ref[...]) for key, ref in where.items()}
    for n, (layer, place) in enumerate(work):
        total = conv_plane(w_ref[layer - 1], [held[layer - 1, place + d] for d in (-1, 0, 1)], acc_ref.at[n % 2])
        if layer == layers:
            store_cells(refs[len(kept)], place - first, where[0, place][...] + total)
            continue
        total = gelu(total)
        held[layer, place] = halves(total)
        if (layer, place) in kept_at:
            kept_at[layer, place][...] = total


def mlp_kernel(y_ref, a_ref, b_ref, out_ref, hh_ref, hl_ref):
    channels = y_ref.shape[0]
    hidden = hh_ref.shape[0]
    rows = 256
    y = y_ref[...]
    scale = lax.rsqrt(jnp.mean(y * y, axis=0, keepdims=True) + 1e-06)
    hi, lo = halves(y * scale)
    seen = jnp.concatenate([hi, lo, hi], axis=0)
    for r in range(0, hidden, rows):
        top, low = a_ref[r : r + rows, :], a_ref[hidden + r : hidden + r + rows, :]
        hid = gelu(jnp.dot(jnp.concatenate([top, top, low], axis=1), seen, preferred_element_type=F32))
        hh, hl = halves(hid)
        hh_ref[r : r + rows, :] = hh
        hl_ref[r : r + rows, :] = hl
    seen = jnp.concatenate([hh_ref[...], hl_ref[...], hh_ref[...]], axis=0)
    for r in range(0, channels, rows):
        top, low = b_ref[r : r + rows, :], b_ref[channels + r : channels + r + rows, :]
        part = jnp.concatenate([top, top, low], axis=1)
        out_ref[r : r + rows, :] = y_ref[r : r + rows, :] + jnp.dot(part, seen, preferred_element_type=F32)


def place_kernel(in_ref, out_hbm, held_ref, sems):
    size = in_ref.shape[2]
    width, planes, cells = out_hbm.shape
    runs = cells // size
    flip = turned_here()
    rows = width // sems.shape[0]
    copies = []
    for n in range(width // rows):
        part = slice(n * rows, (n + 1) * rows)
        for p in range(planes):
            start = jnp.where(flip, planes - 1 - p, p) * runs
            pieces = [in_ref[start + q, part, v : v + 128] for q in range(runs) for v in range(0, size, 128)]
            for v, piece in enumerate(rearranged(pieces, True)):
                held_ref[part, p, v * 128 : (v + 1) * 128] = piece
        part = pl.ds(n * rows, rows)
        copies.append(pltpu.make_async_copy(held_ref.at[part], out_hbm.at[part], sems.at[n]))
        copies[-1].start()
    for copy in copies:
        copy.wait()


def per_device(volume, conv_weight, norm_gain, mlp_in, mlp_out):
    width, planes, cells = volume.shape
    count = lax.axis_size("depth")
    members = lax.axis_size("chan")
    kernels = conv_weight[0, :, 0]
    layers = kernels.shape[0]
    channels, hidden = mlp_out.shape[1], mlp_out.shape[2]
    size = planes * cells // members
    plane = jax.ShapeDtypeStruct((width, cells), F32)

    pair = [(i, i ^ 1) for i in range(count)]
    along = [(i, (i + (2 if i % 2 == 0 else count - 2)) % count) for i in range(count)]
    own = []
    for places in ((0,), tuple(range(1, planes))):
        body = functools.partial(planes_kernel, places)
        own += call(
            body,
            (plane,) * len(places),
            10**9,
            len(places) * width * cells * 8,
            [HBM],
            [pltpu.VMEM((len(places), width, cells), F32), pltpu.SemaphoreType.DMA((len(places),))],
        )(pltpu.with_memory_space_constraint(volume, pltpu.HBM))
    there = [lax.ppermute(q, "depth", pair) for q in own[:2]]
    taps = call(
        taps_kernel,
        jax.ShapeDtypeStruct((layers, 9 * width, 384), BF16),
        0,
        kernels.size * 8,
        [VMEM],
        [pltpu.VMEM((width, 1024), F32)],
    )(kernels)
    held = {(0, 3 + k): v for k, v in enumerate(own)}

    def stage(given, work, kept, finished=None):
        outs = (plane,) * len(kept)
        if any(layer == layers for layer, _ in work):
            outs += (jax.ShapeDtypeStruct((members, width, size), F32),)
        more = [] if finished is None else [finished]
        got = call(
            functools.partial(stage_kernel, given, work, kept, layers, len(more)),
            outs,
            len(work) * 2 * 288 * 384 * cells,
            (len(given) + len(outs)) * width * cells * 4,
            [VMEM] * (1 + len(given) + len(more)),
            [pltpu.VMEM((2, 9 * width, cells), F32)],
            {1 + len(given): len(kept)} if more else None,
        )(taps, *[held[key] for key in given], *more)
        held.update(zip(kept, got))
        return got[-1]

    stage(((0, 3), (0, 4), (0, 5), (0, 6)), ((1, 4), (1, 5)), ((1, 4), (1, 5)))
    weights = jax.ShapeDtypeStruct((2 * hidden, channels), BF16)
    w_in = call(first_weights_kernel, weights, 0, mlp_in.size * 8, [VMEM] * 2)(norm_gain, mlp_in[0])
    third, held[1, 4], held[1, 5] = lax.optimization_barrier((own[2], held[1, 4], held[1, 5]))
    weights = jax.ShapeDtypeStruct((2 * channels, hidden), BF16)
    w_out = call(second_weights_kernel, weights, 0, mlp_out.size * 8, [VMEM])(mlp_out[0])
    fourth, w_out = lax.optimization_barrier((own[3], w_out))
    there[1], w_in = lax.optimization_barrier((there[1], w_in))
    there += [lax.ppermute(q, "depth", pair) for q in (third, fourth)]
    for k in range(layers):
        held[0, 2 - k] = lax.ppermute(there[k], "depth", along)
        held[0, 9 - k] = there[k + 1]
    stage(((0, 2), (0, 3), (0, 4), (1, 4), (1, 5)), ((1, 3), (2, 4)), ((1, 3), (2, 4)))
    most = stage(
        ((0, 5), (0, 6), (0, 7), (0, 8), (0, 9), (1, 4), (1, 5), (2, 4)),
        ((1, 6), (1, 7), (1, 8), (2, 5), (2, 6), (2, 7), (3, 5), (3, 6)),
        ((2, 5),),
    )
    mixed = stage(
        ((0, 0), (0, 1), (0, 2), (0, 3), (0, 4), (1, 3), (1, 4), (2, 4), (2, 5)),
        ((1, 2), (1, 1), (2, 3), (2, 2), (3, 4), (3, 3)),
        (),
        most,
    )
    here = lax.all_to_all(mixed, "chan", split_axis=0, concat_axis=0, tiled=True)
    out = call(
        mlp_kernel,
        jax.ShapeDtypeStruct((channels, size), F32),
        12 * hidden * channels * size,
        mlp_in.size * 8,
        [VMEM] * 3,
        [pltpu.VMEM((hidden, size), BF16)] * 2,
    )(here.reshape(channels, size), w_in, w_out)
    back = lax.all_to_all(out.reshape(members, width, size), "chan", split_axis=0, concat_axis=0, tiled=True)
    return call(
        place_kernel,
        jax.ShapeDtypeStruct(volume.shape, F32),
        0,
        volume.size * 8,
        [VMEM],
        [pltpu.VMEM(volume.shape, F32), pltpu.SemaphoreType.DMA((PARTS,))],
        outs_in=HBM,
    )(back)


def solution(mesh):
    in_specs = (P("chan", "depth", None), P(None, None, "chan", None, None), P(), P(), P())
    out_specs = P("chan", "depth", None)
    return jax.shard_map(
        per_device, mesh=mesh, in_specs=in_specs, out_specs=out_specs, check_vma=False
    )
```

```python
import functools

import jax
import jax.numpy as jnp
from jax import lax
from jax.experimental import pallas as pl
from jax.experimental.pallas import tpu as pltpu
from jax.sharding import PartitionSpec as P

W = 32
PARTS = 4
F32 = jnp.float32
BF16 = jnp.bfloat16
VMEM = pl.BlockSpec(memory_space=pltpu.VMEM)
HBM = pl.BlockSpec(memory_space=pltpu.HBM)


def call(body, outs, flops, moved, ins, scratch=(), aliases=None, outs_in=VMEM):
    return pl.pallas_call(
        body,
        out_shape=outs,
        in_specs=ins,
        out_specs=jax.tree.map(lambda _: outs_in, outs),
        scratch_shapes=scratch,
        input_output_aliases=aliases or {},
        cost_estimate=pl.CostEstimate(flops=flops, bytes_accessed=moved, transcendentals=0),
        compiler_params=pltpu.CompilerParams(vmem_limit_bytes=32 << 20),
    )


def halves(x):
    hi = x.astype(BF16)
    return hi, (x - hi.astype(F32)).astype(BF16)


def gelu(v):
    return 0.5 * v * (1.0 + jnp.tanh(0.7978845608028654 * (v + 0.044715 * (v * v * v))))


def turned_here():
    return lax.axis_index("depth") % 2 > 0


def rearranged(pieces, back):
    block = lax.broadcasted_iota(jnp.int32, pieces[0].shape, 1) // W
    count = len(pieces)
    runs = 128 // W
    half = count // runs
    moved = [None] * count
    for s in range(half):
        group = [pieces[s * runs + n] if back else pieces[n * half + s] for n in range(runs)]
        step = runs // 2
        while step:
            lower = block // step % 2 == 0
            for n in range(runs):
                if n // step % 2 == 0:
                    a, b = group[n], group[n + step]
                    group[n] = jnp.where(lower, a, pltpu.roll(b, step * W, 1))
                    group[n + step] = jnp.where(lower, pltpu.roll(a, 128 - step * W, 1), b)
            step //= 2
        for n in range(runs):
            moved[n * half + s if back else s * runs + n] = group[n]
    return moved


def planes_kernel(places, x_ref, *q_refs):
    last = x_ref.shape[1] - 1
    flip = turned_here()
    for k, q_ref in zip(places, q_refs, strict=True):
        plane = jnp.where(flip, x_ref[:, last - k, :], x_ref[:, k, :])
        pieces = [plane[:, v : v + 128] for v in range(0, plane.shape[1], 128)]
        q_ref[...] = jnp.concatenate(rearranged(pieces, False), axis=1)


def taps_kernel(k_ref, w_ref, pad_ref):
    layers, width, taps = k_ref.shape
    flip = turned_here()
    lane = lax.broadcasted_iota(jnp.int32, (width, 128), 1)
    pad_ref[...] = jnp.zeros_like(pad_ref)
    for layer in range(layers):
        pad_ref[:, :taps] = k_ref[layer]
        for tap in range(9):
            start = tap * 3 * width
            base, shift = start // 128 * 128, start % 128
            pair = pad_ref[:, base : base + 256]
            if shift:
                pair = pltpu.roll(pair, 256 - shift, 1)
            ahead = pair[:, :128]
            turned = jnp.where(lane // width == 1, ahead, pltpu.roll(ahead, 2 * width, 1))
            hi, lo = halves(jnp.where(lane < 3 * width, jnp.where(flip, turned, ahead), 0.0))
            rows = pl.ds(tap * width, width)
            w_ref[layer, rows, 0:128] = hi
            w_ref[layer, rows, 128:256] = hi
            w_ref[layer, rows, 256:384] = lo


def first_weights_kernel(gain_ref, a_ref, w_ref):
    gain = gain_ref[...]
    hidden = a_ref.shape[0]
    rows = 128
    for r in range(0, hidden, rows):
        hi, lo = halves(a_ref[r : r + rows, :] * gain)
        w_ref[r : r + rows, :] = hi
        w_ref[hidden + r : hidden + r + rows, :] = lo


def second_weights_kernel(b_ref, w_ref):
    channels = b_ref.shape[0]
    rows = 128
    for r in range(0, channels, rows):
        hi, lo = halves(b_ref[r : r + rows, :])
        w_ref[r : r + rows, :] = hi
        w_ref[channels + r : channels + r + rows, :] = lo


def tiles(pieces):
    return [halves(jnp.concatenate(pieces[n : n + 2], axis=1)) for n in range(0, len(pieces), 2)]


def split(plane):
    return [plane[:, v : v + 128] for v in range(0, plane.shape[1], 128)]


def conv_plane(weight, three, acc_ref):
    width, size = three[0][0][0].shape
    zero = jnp.zeros((width, size), BF16)
    count = acc_ref.shape[1] // 128
    column = lax.broadcasted_iota(jnp.int32, (width, 128), 1) % W

    def tap(b, c, v):
        return acc_ref[(b * 3 + c) * width : (b * 3 + c + 1) * width, v * 128 : (v + 1) * 128]

    def rows(c, v):
        above = tap(0, c, v - 1) if v else pltpu.roll(tap(0, c, count - 1), W, 1)
        below = tap(2, c, v + 1) if v < count - 1 else pltpu.roll(tap(2, c, 0), 128 - W, 1)
        return tap(1, c, v) + above + below

    ready = set()
    parts = [None] * count
    last = len(three[0]) - 1
    for n in (last, *range(last)):
        his = [t[n][0] for t in three] + [zero]
        los = [t[n][1] for t in three] + [zero]
        acc_ref[:, n * size : (n + 1) * size] = jnp.dot(
            weight, jnp.concatenate(his + los + his, axis=0), preferred_element_type=F32
        )
        ready |= {n * size // 128, n * size // 128 + 1}
        for v in range(count):
            if parts[v] is not None or not {(v - 1) % count, v, (v + 1) % count} <= ready:
                continue
            left, here, right = (rows(c, v) for c in range(3))
            left = jnp.where(column == 0, pltpu.roll(left, 128 - W + 1, 1), pltpu.roll(left, 1, 1))
            right = jnp.where(column == W - 1, pltpu.roll(right, W - 1, 1), pltpu.roll(right, 127, 1))
            parts[v] = left + here + right
    return parts


def store_cells(out_ref, plane, pieces):
    size = out_ref.shape[2]
    each = size // 128
    for v, piece in enumerate(pieces):
        at = v % each * 128
        out_ref[plane * (len(pieces) // each) + v // each, :, at : at + 128] = piece


def stage_kernel(given, work, kept, first, resumes, w_ref, *refs):
    ins, refs = refs[: len(given)], refs[len(given) :]
    acc_ref = refs[-1]
    layers = w_ref.shape[0]
    refs = refs[resumes:]
    where = dict(zip(given, ins, strict=True))
    kept_at = dict(zip(kept, refs[: len(kept)], strict=True))
    held = {key: tiles(split(ref[...])) for key, ref in where.items()}
    for n, (layer, place) in enumerate(work):
        pieces = conv_plane(w_ref[layer - 1], [held[layer - 1, place + d] for d in (-1, 0, 1)], acc_ref.at[n % 4])
        if layer == layers:
            base = split(where[0, place][...])
            store_cells(refs[len(kept)], place - first, [b + t for b, t in zip(base, pieces, strict=True)])
            continue
        pieces = [gelu(t) for t in pieces]
        held[layer, place] = tiles(pieces)
        if (layer, place) in kept_at:
            for v, piece in enumerate(pieces):
                kept_at[layer, place][:, v * 128 : (v + 1) * 128] = piece


def mlp_kernel(y_ref, a_ref, b_ref, out_ref, hh_ref, hl_ref):
    channels = y_ref.shape[0]
    hidden = hh_ref.shape[0]
    rows = 256
    y = y_ref[...]
    scale = lax.rsqrt(jnp.mean(y * y, axis=0, keepdims=True) + 1e-06)
    hi, lo = halves(y * scale)
    seen = jnp.concatenate([hi, lo, hi], axis=0)
    for r in range(0, hidden, rows):
        top, low = a_ref[r : r + rows, :], a_ref[hidden + r : hidden + r + rows, :]
        hid = gelu(jnp.dot(jnp.concatenate([top, top, low], axis=1), seen, preferred_element_type=F32))
        hh, hl = halves(hid)
        hh_ref[r : r + rows, :] = hh
        hl_ref[r : r + rows, :] = hl
    seen = jnp.concatenate([hh_ref[...], hl_ref[...], hh_ref[...]], axis=0)
    for r in range(0, channels, rows):
        top, low = b_ref[r : r + rows, :], b_ref[channels + r : channels + r + rows, :]
        part = jnp.concatenate([top, top, low], axis=1)
        out_ref[r : r + rows, :] = y_ref[r : r + rows, :] + jnp.dot(part, seen, preferred_element_type=F32)


def place_kernel(in_ref, out_hbm, held_ref, sems):
    size = in_ref.shape[2]
    width, planes, cells = out_hbm.shape
    runs = cells // size
    flip = turned_here()
    rows = width // sems.shape[0]
    copies = []
    for n in range(width // rows):
        part = slice(n * rows, (n + 1) * rows)
        for p in range(planes):
            start = jnp.where(flip, planes - 1 - p, p) * runs
            pieces = [in_ref[start + q, part, v : v + 128] for q in range(runs) for v in range(0, size, 128)]
            for v, piece in enumerate(rearranged(pieces, True)):
                held_ref[part, p, v * 128 : (v + 1) * 128] = piece
        part = pl.ds(n * rows, rows)
        copies.append(pltpu.make_async_copy(held_ref.at[part], out_hbm.at[part], sems.at[n]))
        copies[-1].start()
    for copy in copies:
        copy.wait()


def per_device(volume, conv_weight, norm_gain, mlp_in, mlp_out):
    width, planes, cells = volume.shape
    count = lax.axis_size("depth")
    members = lax.axis_size("chan")
    kernels = conv_weight[0, :, 0]
    layers = kernels.shape[0]
    channels, hidden = mlp_out.shape[1], mlp_out.shape[2]
    size = planes * cells // members
    plane = jax.ShapeDtypeStruct((width, cells), F32)

    pair = [(i, i ^ 1) for i in range(count)]
    along = [(i, (i + (2 if i % 2 == 0 else count - 2)) % count) for i in range(count)]
    own = []
    for places in ((0,), tuple(range(1, planes))):
        body = functools.partial(planes_kernel, places)
        own += call(body, (plane,) * len(places), 10**9, len(places) * width * cells * 8, [VMEM])(volume)
    there = [lax.ppermute(q, "depth", pair) for q in own[:2]]
    taps = call(
        taps_kernel,
        jax.ShapeDtypeStruct((layers, 9 * width, 384), BF16),
        0,
        kernels.size * 8,
        [VMEM],
        [pltpu.VMEM((width, 1024), F32)],
    )(kernels)
    held = {(0, 3 + k): v for k, v in enumerate(own)}

    def stage(given, work, kept, finished=None):
        outs = (plane,) * len(kept)
        if any(layer == layers for layer, _ in work):
            outs += (jax.ShapeDtypeStruct((members, width, size), F32),)
        more = [] if finished is None else [finished]
        got = call(
            functools.partial(stage_kernel, given, work, kept, layers, len(more)),
            outs,
            len(work) * 2 * 288 * 384 * cells,
            (len(given) + len(outs)) * width * cells * 4,
            [VMEM] * (1 + len(given) + len(more)),
            [pltpu.VMEM((4, 9 * width, cells), F32)],
            {1 + len(given): len(kept)} if more else None,
        )(taps, *[held[key] for key in given], *more)
        held.update(zip(kept, got))
        return got[-1]

    stage(((0, 3), (0, 4), (0, 5), (0, 6)), ((1, 4), (1, 5)), ((1, 4), (1, 5)))
    weights = jax.ShapeDtypeStruct((2 * hidden, channels), BF16)
    w_in = call(first_weights_kernel, weights, 0, mlp_in.size * 8, [VMEM] * 2)(norm_gain, mlp_in[0])
    third, held[1, 4], held[1, 5] = lax.optimization_barrier((own[2], held[1, 4], held[1, 5]))
    weights = jax.ShapeDtypeStruct((2 * channels, hidden), BF16)
    w_out = call(second_weights_kernel, weights, 0, mlp_out.size * 8, [VMEM])(mlp_out[0])
    fourth, w_out = lax.optimization_barrier((own[3], w_out))
    there[1], w_in = lax.optimization_barrier((there[1], w_in))
    there += [lax.ppermute(q, "depth", pair) for q in (third, fourth)]
    for k in range(layers):
        held[0, 2 - k] = lax.ppermute(there[k], "depth", along)
        held[0, 9 - k] = there[k + 1]
    stage(((0, 2), (0, 3), (0, 4), (1, 4), (1, 5)), ((1, 3), (2, 4)), ((1, 3), (2, 4)))
    most = stage(
        ((0, 5), (0, 6), (0, 7), (0, 8), (0, 9), (1, 4), (1, 5), (2, 4)),
        ((1, 6), (1, 7), (1, 8), (2, 5), (2, 6), (2, 7), (3, 5), (3, 6)),
        ((2, 5),),
    )
    mixed = stage(
        ((0, 0), (0, 1), (0, 2), (0, 3), (0, 4), (1, 3), (1, 4), (2, 4), (2, 5)),
        ((1, 2), (1, 1), (2, 3), (2, 2), (3, 4), (3, 3)),
        (),
        most,
    )
    here = lax.all_to_all(mixed, "chan", split_axis=0, concat_axis=0, tiled=True)
    out = call(
        mlp_kernel,
        jax.ShapeDtypeStruct((channels, size), F32),
        12 * hidden * channels * size,
        mlp_in.size * 8,
        [VMEM] * 3,
        [pltpu.VMEM((hidden, size), BF16)] * 2,
    )(here.reshape(channels, size), w_in, w_out)
    back = lax.all_to_all(out.reshape(members, width, size), "chan", split_axis=0, concat_axis=0, tiled=True)
    return call(
        place_kernel,
        jax.ShapeDtypeStruct(volume.shape, F32),
        0,
        volume.size * 8,
        [VMEM],
        [pltpu.VMEM(volume.shape, F32), pltpu.SemaphoreType.DMA((PARTS,))],
        outs_in=HBM,
    )(back)


def solution(mesh):
    in_specs = (P("chan", "depth", None), P(None, None, "chan", None, None), P(), P(), P())
    out_specs = P("chan", "depth", None)
    return jax.shard_map(
        per_device, mesh=mesh, in_specs=in_specs, out_specs=out_specs, check_vma=False
    )
```

```python
import functools

import jax
import jax.numpy as jnp
from jax import lax
from jax.experimental import pallas as pl
from jax.experimental.pallas import tpu as pltpu
from jax.sharding import PartitionSpec as P

W = 32
PARTS = 4
F32 = jnp.float32
BF16 = jnp.bfloat16
VMEM = pl.BlockSpec(memory_space=pltpu.VMEM)
HBM = pl.BlockSpec(memory_space=pltpu.HBM)


def call(body, outs, flops, moved, ins, scratch=(), aliases=None, outs_in=VMEM):
    return pl.pallas_call(
        body,
        out_shape=outs,
        in_specs=ins,
        out_specs=jax.tree.map(lambda _: outs_in, outs),
        scratch_shapes=scratch,
        input_output_aliases=aliases or {},
        cost_estimate=pl.CostEstimate(flops=flops, bytes_accessed=moved, transcendentals=0),
        compiler_params=pltpu.CompilerParams(vmem_limit_bytes=32 << 20),
    )


def halves(x):
    hi = x.astype(BF16)
    return hi, (x - hi.astype(F32)).astype(BF16)


def gelu(v):
    return 0.5 * v * (1.0 + jnp.tanh(0.7978845608028654 * (v + 0.044715 * (v * v * v))))


def turned_here():
    return lax.axis_index("depth") % 2 > 0


def rearranged(pieces, back):
    block = lax.broadcasted_iota(jnp.int32, pieces[0].shape, 1) // W
    count = len(pieces)
    runs = 128 // W
    moved = []
    for v in range(count):
        total = None
        for b in range(runs):
            if back:
                row = v * runs + b
                source, at = row % count, row // count
            else:
                row = b * count + v
                source, at = row // runs, row % runs
            piece = pieces[source]
            if at != b:
                piece = pltpu.roll(piece, (b - at) * W % 128, 1)
            total = piece if total is None else jnp.where(block == b, piece, total)
        moved.append(total)
    return moved


def planes_kernel(places, x_ref, *q_refs):
    last = x_ref.shape[1] - 1
    flip = turned_here()
    for k, q_ref in zip(places, q_refs, strict=True):
        plane = jnp.where(flip, x_ref[:, last - k, :], x_ref[:, k, :])
        pieces = [plane[:, v : v + 128] for v in range(0, plane.shape[1], 128)]
        q_ref[...] = jnp.concatenate(rearranged(pieces, False), axis=1)


def taps_kernel(k_ref, w_ref, pad_ref):
    layers, width, taps = k_ref.shape
    flip = turned_here()
    lane = lax.broadcasted_iota(jnp.int32, (width, 128), 1)
    pad_ref[...] = jnp.zeros_like(pad_ref)
    for layer in range(layers):
        pad_ref[:, :taps] = k_ref[layer]
        for tap in range(9):
            start = tap * 3 * width
            base, shift = start // 128 * 128, start % 128
            pair = pad_ref[:, base : base + 256]
            if shift:
                pair = pltpu.roll(pair, 256 - shift, 1)
            ahead = pair[:, :128]
            turned = jnp.where(lane // width == 1, ahead, pltpu.roll(ahead, 2 * width, 1))
            hi, lo = halves(jnp.where(lane < 3 * width, jnp.where(flip, turned, ahead), 0.0))
            rows = pl.ds(tap * width, width)
            w_ref[layer, rows, 0:128] = hi
            w_ref[layer, rows, 128:256] = hi
            w_ref[layer, rows, 256:384] = lo


def first_weights_kernel(gain_ref, a_ref, w_ref):
    gain = gain_ref[...]
    hidden = a_ref.shape[0]
    rows = 128
    for r in range(0, hidden, rows):
        hi, lo = halves(a_ref[r : r + rows, :] * gain)
        w_ref[r : r + rows, :] = hi
        w_ref[hidden + r : hidden + r + rows, :] = lo


def second_weights_kernel(b_ref, w_ref):
    channels = b_ref.shape[0]
    rows = 128
    for r in range(0, channels, rows):
        hi, lo = halves(b_ref[r : r + rows, :])
        w_ref[r : r + rows, :] = hi
        w_ref[channels + r : channels + r + rows, :] = lo


def conv_plane(weight, three, acc_ref):
    zero = jnp.zeros_like(three[0][0])
    his = [t[0] for t in three] + [zero]
    los = [t[1] for t in three] + [zero]
    acc_ref[...] = jnp.dot(weight, jnp.concatenate(his + los + his, axis=0), preferred_element_type=F32)
    width, cells = zero.shape
    count = cells // 128

    def tap(b, c, v):
        return acc_ref[(b * 3 + c) * width : (b * 3 + c + 1) * width, v * 128 : (v + 1) * 128]

    def rows(c, v):
        above = tap(0, c, v - 1) if v else pltpu.roll(tap(0, c, count - 1), W, 1)
        below = tap(2, c, v + 1) if v < count - 1 else pltpu.roll(tap(2, c, 0), 128 - W, 1)
        return tap(1, c, v) + above + below

    column = lax.broadcasted_iota(jnp.int32, (width, 128), 1) % W
    parts = []
    for v in range(count):
        left, here, right = (rows(c, v) for c in range(3))
        left = jnp.where(column == 0, pltpu.roll(left, 128 - W + 1, 1), pltpu.roll(left, 1, 1))
        right = jnp.where(column == W - 1, pltpu.roll(right, W - 1, 1), pltpu.roll(right, 127, 1))
        parts.append(left + here + right)
    return jnp.concatenate(parts, axis=1)


def store_cells(out_ref, plane, value):
    size = out_ref.shape[2]
    runs = value.shape[1] // size
    for q in range(runs):
        out_ref[plane * runs + q] = value[:, q * size : (q + 1) * size]


def stage_kernel(given, work, kept, first, resumes, w_ref, *refs):
    ins, refs = refs[: len(given)], refs[len(given) :]
    acc_ref = refs[-1]
    layers = w_ref.shape[0]
    refs = refs[resumes:]
    where = dict(zip(given, ins, strict=True))
    kept_at = dict(zip(kept, refs[: len(kept)], strict=True))
    held = {key: halves(ref[...]) for key, ref in where.items()}
    for n, (layer, place) in enumerate(work):
        total = conv_plane(w_ref[layer - 1], [held[layer - 1, place + d] for d in (-1, 0, 1)], acc_ref.at[n % 2])
        if layer == layers:
            store_cells(refs[len(kept)], place - first, where[0, place][...] + total)
            continue
        total = gelu(total)
        held[layer, place] = halves(total)
        if (layer, place) in kept_at:
            kept_at[layer, place][...] = total


def mlp_kernel(y_ref, a_ref, b_ref, out_ref, hh_ref, hl_ref):
    channels = y_ref.shape[0]
    hidden = hh_ref.shape[0]
    rows = 256
    y = y_ref[...]
    scale = lax.rsqrt(jnp.mean(y * y, axis=0, keepdims=True) + 1e-06)
    hi, lo = halves(y * scale)
    seen = jnp.concatenate([hi, lo, hi], axis=0)
    for r in range(0, hidden, rows):
        top, low = a_ref[r : r + rows, :], a_ref[hidden + r : hidden + r + rows, :]
        hid = gelu(jnp.dot(jnp.concatenate([top, top, low], axis=1), seen, preferred_element_type=F32))
        hh, hl = halves(hid)
        hh_ref[r : r + rows, :] = hh
        hl_ref[r : r + rows, :] = hl
    seen = jnp.concatenate([hh_ref[...], hl_ref[...], hh_ref[...]], axis=0)
    for r in range(0, channels, rows):
        top, low = b_ref[r : r + rows, :], b_ref[channels + r : channels + r + rows, :]
        part = jnp.concatenate([top, top, low], axis=1)
        out_ref[r : r + rows, :] = y_ref[r : r + rows, :] + jnp.dot(part, seen, preferred_element_type=F32)


def place_kernel(in_ref, out_hbm, held_ref, sems):
    size = in_ref.shape[2]
    width, planes, cells = out_hbm.shape
    runs = cells // size
    flip = turned_here()
    rows = width // sems.shape[0]
    copies = []
    for n in range(width // rows):
        part = slice(n * rows, (n + 1) * rows)
        for p in range(planes):
            start = jnp.where(flip, planes - 1 - p, p) * runs
            pieces = [in_ref[start + q, part, v : v + 128] for q in range(runs) for v in range(0, size, 128)]
            for v, piece in enumerate(rearranged(pieces, True)):
                held_ref[part, p, v * 128 : (v + 1) * 128] = piece
        part = pl.ds(n * rows, rows)
        copies.append(pltpu.make_async_copy(held_ref.at[part], out_hbm.at[part], sems.at[n]))
        copies[-1].start()
    for copy in copies:
        copy.wait()


def per_device(volume, conv_weight, norm_gain, mlp_in, mlp_out):
    width, planes, cells = volume.shape
    count = lax.axis_size("depth")
    members = lax.axis_size("chan")
    kernels = conv_weight[0, :, 0]
    layers = kernels.shape[0]
    channels, hidden = mlp_out.shape[1], mlp_out.shape[2]
    size = planes * cells // members
    plane = jax.ShapeDtypeStruct((width, cells), F32)

    pair = [(i, i ^ 1) for i in range(count)]
    along = [(i, (i + (2 if i % 2 == 0 else count - 2)) % count) for i in range(count)]
    own = []
    for places in ((0,), tuple(range(1, planes))):
        body = functools.partial(planes_kernel, places)
        own += call(body, (plane,) * len(places), 10**9, len(places) * width * cells * 8, [VMEM])(volume)
    there = [lax.ppermute(q, "depth", pair) for q in own[:2]]
    taps = call(
        taps_kernel,
        jax.ShapeDtypeStruct((layers, 9 * width, 384), BF16),
        0,
        kernels.size * 8,
        [VMEM],
        [pltpu.VMEM((width, 1024), F32)],
    )(kernels)
    held = {(0, 3 + k): v for k, v in enumerate(own)}

    def stage(given, work, kept, finished=None):
        outs = (plane,) * len(kept)
        if any(layer == layers for layer, _ in work):
            outs += (jax.ShapeDtypeStruct((members, width, size), F32),)
        more = [] if finished is None else [finished]
        got = call(
            functools.partial(stage_kernel, given, work, kept, layers, len(more)),
            outs,
            len(work) * 2 * 288 * 384 * cells,
            (len(given) + len(outs)) * width * cells * 4,
            [VMEM] * (1 + len(given) + len(more)),
            [pltpu.VMEM((2, 9 * width, cells), F32)],
            {1 + len(given): len(kept)} if more else None,
        )(taps, *[held[key] for key in given], *more)
        held.update(zip(kept, got))
        return got[-1]

    stage(((0, 3), (0, 4), (0, 5), (0, 6)), ((1, 4), (1, 5)), ((1, 4), (1, 5)))
    weights = jax.ShapeDtypeStruct((2 * hidden, channels), BF16)
    w_in = call(first_weights_kernel, weights, 0, mlp_in.size * 8, [VMEM] * 2)(norm_gain, mlp_in[0])
    third, held[1, 4], held[1, 5], w_in = lax.optimization_barrier((own[2], held[1, 4], held[1, 5], w_in))
    weights = jax.ShapeDtypeStruct((2 * channels, hidden), BF16)
    w_out = call(second_weights_kernel, weights, 0, mlp_out.size * 8, [VMEM])(mlp_out[0])
    fourth, w_out = lax.optimization_barrier((own[3], w_out))
    there[1], w_out = lax.optimization_barrier((there[1], w_out))
    there += [lax.ppermute(q, "depth", pair) for q in (third, fourth)]
    for k in range(layers):
        held[0, 2 - k] = lax.ppermute(there[k], "depth", along)
        held[0, 9 - k] = there[k + 1]
    stage(((0, 2), (0, 3), (0, 4), (1, 4), (1, 5)), ((1, 3), (2, 4)), ((1, 3), (2, 4)))
    most = stage(
        ((0, 5), (0, 6), (0, 7), (0, 8), (0, 9), (1, 4), (1, 5), (2, 4)),
        ((1, 6), (1, 7), (1, 8), (2, 5), (2, 6), (2, 7), (3, 5), (3, 6)),
        ((2, 5),),
    )
    mixed = stage(
        ((0, 0), (0, 1), (0, 2), (0, 3), (0, 4), (1, 3), (1, 4), (2, 4), (2, 5)),
        ((1, 2), (1, 1), (2, 3), (2, 2), (3, 4), (3, 3)),
        (),
        most,
    )
    here = lax.all_to_all(mixed, "chan", split_axis=0, concat_axis=0, tiled=True)
    out = call(
        mlp_kernel,
        jax.ShapeDtypeStruct((channels, size), F32),
        12 * hidden * channels * size,
        mlp_in.size * 8,
        [VMEM] * 3,
        [pltpu.VMEM((hidden, size), BF16)] * 2,
    )(here.reshape(channels, size), w_in, w_out)
    back = lax.all_to_all(out.reshape(members, width, size), "chan", split_axis=0, concat_axis=0, tiled=True)
    return call(
        place_kernel,
        jax.ShapeDtypeStruct(volume.shape, F32),
        0,
        volume.size * 8,
        [VMEM],
        [pltpu.VMEM(volume.shape, F32), pltpu.SemaphoreType.DMA((PARTS,))],
        outs_in=HBM,
    )(back)


def solution(mesh):
    in_specs = (P("chan", "depth", None), P(None, None, "chan", None, None), P(), P(), P())
    out_specs = P("chan", "depth", None)
    return jax.shard_map(
        per_device, mesh=mesh, in_specs=in_specs, out_specs=out_specs, check_vma=False
    )
```

```python
import functools

import jax
import jax.numpy as jnp
from jax import lax
from jax.experimental import pallas as pl
from jax.experimental.pallas import tpu as pltpu
from jax.sharding import PartitionSpec as P

W = 32
PARTS = 4
F32 = jnp.float32
BF16 = jnp.bfloat16
VMEM = pl.BlockSpec(memory_space=pltpu.VMEM)
HBM = pl.BlockSpec(memory_space=pltpu.HBM)


def call(body, outs, flops, moved, ins, scratch=(), aliases=None, outs_in=VMEM):
    return pl.pallas_call(
        body,
        out_shape=outs,
        in_specs=ins,
        out_specs=jax.tree.map(lambda _: outs_in, outs),
        scratch_shapes=scratch,
        input_output_aliases=aliases or {},
        cost_estimate=pl.CostEstimate(flops=flops, bytes_accessed=moved, transcendentals=0),
        compiler_params=pltpu.CompilerParams(vmem_limit_bytes=32 << 20),
    )


def halves(x):
    hi = x.astype(BF16)
    return hi, (x - hi.astype(F32)).astype(BF16)


def gelu(v):
    return 0.5 * v * (1.0 + jnp.tanh(0.7978845608028654 * (v + 0.044715 * (v * v * v))))


def turned_here():
    return lax.axis_index("depth") % 2 > 0


def rearranged(pieces, back):
    block = lax.broadcasted_iota(jnp.int32, pieces[0].shape, 1) // W
    count = len(pieces)
    runs = 128 // W
    moved = []
    for v in range(count):
        total = None
        for b in range(runs):
            if back:
                row = v * runs + b
                source, at = row % count, row // count
            else:
                row = b * count + v
                source, at = row // runs, row % runs
            piece = pieces[source]
            if at != b:
                piece = pltpu.roll(piece, (b - at) * W % 128, 1)
            total = piece if total is None else jnp.where(block == b, piece, total)
        moved.append(total)
    return moved


def first_plane_kernel(x_hbm, x_ref, q_ref, sems):
    rows = x_ref.shape[0] // PARTS
    copies = []
    for n in range(PARTS):
        part = pl.ds(n * rows, rows)
        copies.append(pltpu.make_async_copy(x_hbm.at[part], x_ref.at[part], sems.at[n]))
        copies[-1].start()
    for copy in copies:
        copy.wait()
    planes_kernel((0,), x_ref, q_ref)


def planes_kernel(places, x_ref, *q_refs):
    last = x_ref.shape[1] - 1
    flip = turned_here()
    for k, q_ref in zip(places, q_refs, strict=True):
        plane = jnp.where(flip, x_ref[:, last - k, :], x_ref[:, k, :])
        pieces = [plane[:, v : v + 128] for v in range(0, plane.shape[1], 128)]
        q_ref[...] = jnp.concatenate(rearranged(pieces, False), axis=1)


def taps_kernel(k_ref, w_ref, pad_ref):
    layers, width, taps = k_ref.shape
    flip = turned_here()
    lane = lax.broadcasted_iota(jnp.int32, (width, 128), 1)
    pad_ref[...] = jnp.zeros_like(pad_ref)
    for layer in range(layers):
        pad_ref[:, :taps] = k_ref[layer]
        for tap in range(9):
            start = tap * 3 * width
            base, shift = start // 128 * 128, start % 128
            pair = pad_ref[:, base : base + 256]
            if shift:
                pair = pltpu.roll(pair, 256 - shift, 1)
            ahead = pair[:, :128]
            turned = jnp.where(lane // width == 1, ahead, pltpu.roll(ahead, 2 * width, 1))
            hi, lo = halves(jnp.where(lane < 3 * width, jnp.where(flip, turned, ahead), 0.0))
            rows = pl.ds(tap * width, width)
            w_ref[layer, rows, 0:128] = hi
            w_ref[layer, rows, 128:256] = hi
            w_ref[layer, rows, 256:384] = lo


def first_weights_kernel(gain_ref, a_ref, w_ref):
    gain = gain_ref[...]
    hidden = a_ref.shape[0]
    rows = 128
    for r in range(0, hidden, rows):
        hi, lo = halves(a_ref[r : r + rows, :] * gain)
        w_ref[r : r + rows, :] = hi
        w_ref[hidden + r : hidden + r + rows, :] = lo


def second_weights_kernel(b_ref, w_ref):
    channels = b_ref.shape[0]
    rows = 128
    for r in range(0, channels, rows):
        hi, lo = halves(b_ref[r : r + rows, :])
        w_ref[r : r + rows, :] = hi
        w_ref[channels + r : channels + r + rows, :] = lo


def conv_plane(weight, three, acc_ref):
    zero = jnp.zeros_like(three[0][0])
    his = [t[0] for t in three] + [zero]
    los = [t[1] for t in three] + [zero]
    acc_ref[...] = jnp.dot(weight, jnp.concatenate(his + los + his, axis=0), preferred_element_type=F32)
    width, cells = zero.shape
    count = cells // 128

    def tap(b, c, v):
        return acc_ref[(b * 3 + c) * width : (b * 3 + c + 1) * width, v * 128 : (v + 1) * 128]

    def rows(c, v):
        above = tap(0, c, v - 1) if v else pltpu.roll(tap(0, c, count - 1), W, 1)
        below = tap(2, c, v + 1) if v < count - 1 else pltpu.roll(tap(2, c, 0), 128 - W, 1)
        return tap(1, c, v) + above + below

    column = lax.broadcasted_iota(jnp.int32, (width, 128), 1) % W
    parts = []
    for v in range(count):
        left, here, right = (rows(c, v) for c in range(3))
        left = jnp.where(column == 0, pltpu.roll(left, 128 - W + 1, 1), pltpu.roll(left, 1, 1))
        right = jnp.where(column == W - 1, pltpu.roll(right, W - 1, 1), pltpu.roll(right, 127, 1))
        parts.append(left + here + right)
    return jnp.concatenate(parts, axis=1)


def store_cells(out_ref, plane, value):
    size = out_ref.shape[2]
    runs = value.shape[1] // size
    for q in range(runs):
        out_ref[plane * runs + q] = value[:, q * size : (q + 1) * size]


def stage_kernel(given, work, kept, first, resumes, w_ref, *refs):
    ins, refs = refs[: len(given)], refs[len(given) :]
    acc_ref = refs[-1]
    layers = w_ref.shape[0]
    refs = refs[resumes:]
    where = dict(zip(given, ins, strict=True))
    kept_at = dict(zip(kept, refs[: len(kept)], strict=True))
    held = {key: halves(ref[...]) for key, ref in where.items()}
    for n, (layer, place) in enumerate(work):
        total = conv_plane(w_ref[layer - 1], [held[layer - 1, place + d] for d in (-1, 0, 1)], acc_ref.at[n % 2])
        if layer == layers:
            store_cells(refs[len(kept)], place - first, where[0, place][...] + total)
            continue
        total = gelu(total)
        held[layer, place] = halves(total)
        if (layer, place) in kept_at:
            kept_at[layer, place][...] = total


def mlp_kernel(y_ref, a_ref, b_ref, out_ref, hh_ref, hl_ref):
    channels = y_ref.shape[0]
    hidden = hh_ref.shape[0]
    rows = 256
    y = y_ref[...]
    scale = lax.rsqrt(jnp.mean(y * y, axis=0, keepdims=True) + 1e-06)
    hi, lo = halves(y * scale)
    seen = jnp.concatenate([hi, lo, hi], axis=0)
    for r in range(0, hidden, rows):
        top, low = a_ref[r : r + rows, :], a_ref[hidden + r : hidden + r + rows, :]
        hid = gelu(jnp.dot(jnp.concatenate([top, top, low], axis=1), seen, preferred_element_type=F32))
        hh, hl = halves(hid)
        hh_ref[r : r + rows, :] = hh
        hl_ref[r : r + rows, :] = hl
    seen = jnp.concatenate([hh_ref[...], hl_ref[...], hh_ref[...]], axis=0)
    for r in range(0, channels, rows):
        top, low = b_ref[r : r + rows, :], b_ref[channels + r : channels + r + rows, :]
        part = jnp.concatenate([top, top, low], axis=1)
        out_ref[r : r + rows, :] = y_ref[r : r + rows, :] + jnp.dot(part, seen, preferred_element_type=F32)


def place_kernel(in_ref, out_hbm, held_ref, sems):
    size = in_ref.shape[2]
    width, planes, cells = out_hbm.shape
    runs = cells // size
    flip = turned_here()
    rows = width // sems.shape[0]
    copies = []
    for n in range(width // rows):
        part = slice(n * rows, (n + 1) * rows)
        for p in range(planes):
            start = jnp.where(flip, planes - 1 - p, p) * runs
            pieces = [in_ref[start + q, part, v : v + 128] for q in range(runs) for v in range(0, size, 128)]
            for v, piece in enumerate(rearranged(pieces, True)):
                held_ref[part, p, v * 128 : (v + 1) * 128] = piece
        part = pl.ds(n * rows, rows)
        copies.append(pltpu.make_async_copy(held_ref.at[part], out_hbm.at[part], sems.at[n]))
        copies[-1].start()
    for copy in copies:
        copy.wait()


def per_device(volume, conv_weight, norm_gain, mlp_in, mlp_out):
    width, planes, cells = volume.shape
    count = lax.axis_size("depth")
    members = lax.axis_size("chan")
    kernels = conv_weight[0, :, 0]
    layers = kernels.shape[0]
    channels, hidden = mlp_out.shape[1], mlp_out.shape[2]
    size = planes * cells // members
    plane = jax.ShapeDtypeStruct((width, cells), F32)

    pair = [(i, i ^ 1) for i in range(count)]
    along = [(i, (i + (2 if i % 2 == 0 else count - 2)) % count) for i in range(count)]
    here, first = call(
        first_plane_kernel,
        (jax.ShapeDtypeStruct(volume.shape, F32), plane),
        10**9,
        volume.size * 8,
        [HBM],
        [pltpu.SemaphoreType.DMA((PARTS,))],
    )(pltpu.with_memory_space_constraint(volume, pltpu.HBM))
    body = functools.partial(planes_kernel, tuple(range(1, planes)))
    own = (first, *call(body, (plane,) * (planes - 1), 10**9, volume.size * 6, [VMEM])(here))
    there = [lax.ppermute(q, "depth", pair) for q in own[:2]]
    taps = call(
        taps_kernel,
        jax.ShapeDtypeStruct((layers, 9 * width, 384), BF16),
        0,
        kernels.size * 8,
        [VMEM],
        [pltpu.VMEM((width, 1024), F32)],
    )(kernels)
    held = {(0, 3 + k): v for k, v in enumerate(own)}

    def stage(given, work, kept, finished=None):
        outs = (plane,) * len(kept)
        if any(layer == layers for layer, _ in work):
            outs += (jax.ShapeDtypeStruct((members, width, size), F32),)
        more = [] if finished is None else [finished]
        got = call(
            functools.partial(stage_kernel, given, work, kept, layers, len(more)),
            outs,
            len(work) * 2 * 288 * 384 * cells,
            (len(given) + len(outs)) * width * cells * 4,
            [VMEM] * (1 + len(given) + len(more)),
            [pltpu.VMEM((2, 9 * width, cells), F32)],
            {1 + len(given): len(kept)} if more else None,
        )(taps, *[held[key] for key in given], *more)
        held.update(zip(kept, got))
        return got[-1]

    stage(((0, 3), (0, 4), (0, 5), (0, 6)), ((1, 4), (1, 5)), ((1, 4), (1, 5)))
    weights = jax.ShapeDtypeStruct((2 * hidden, channels), BF16)
    w_in = call(first_weights_kernel, weights, 0, mlp_in.size * 8, [VMEM] * 2)(norm_gain, mlp_in[0])
    third, held[1, 4], held[1, 5], w_in = lax.optimization_barrier((own[2], held[1, 4], held[1, 5], w_in))
    weights = jax.ShapeDtypeStruct((2 * channels, hidden), BF16)
    w_out = call(second_weights_kernel, weights, 0, mlp_out.size * 8, [VMEM])(mlp_out[0])
    fourth, w_out = lax.optimization_barrier((own[3], w_out))
    there[1], w_out = lax.optimization_barrier((there[1], w_out))
    there += [lax.ppermute(q, "depth", pair) for q in (third, fourth)]
    for k in range(layers):
        held[0, 2 - k] = lax.ppermute(there[k], "depth", along)
        held[0, 9 - k] = there[k + 1]
    stage(((0, 2), (0, 3), (0, 4), (1, 4), (1, 5)), ((1, 3), (2, 4)), ((1, 3), (2, 4)))
    most = stage(
        ((0, 5), (0, 6), (0, 7), (0, 8), (0, 9), (1, 4), (1, 5), (2, 4)),
        ((1, 6), (1, 7), (1, 8), (2, 5), (2, 6), (2, 7), (3, 5), (3, 6)),
        ((2, 5),),
    )
    mixed = stage(
        ((0, 0), (0, 1), (0, 2), (0, 3), (0, 4), (1, 3), (1, 4), (2, 4), (2, 5)),
        ((1, 2), (1, 1), (2, 3), (2, 2), (3, 4), (3, 3)),
        (),
        most,
    )
    here = lax.all_to_all(mixed, "chan", split_axis=0, concat_axis=0, tiled=True)
    out = call(
        mlp_kernel,
        jax.ShapeDtypeStruct((channels, size), F32),
        12 * hidden * channels * size,
        mlp_in.size * 8,
        [VMEM] * 3,
        [pltpu.VMEM((hidden, size), BF16)] * 2,
    )(here.reshape(channels, size), w_in, w_out)
    back = lax.all_to_all(out.reshape(members, width, size), "chan", split_axis=0, concat_axis=0, tiled=True)
    return call(
        place_kernel,
        jax.ShapeDtypeStruct(volume.shape, F32),
        0,
        volume.size * 8,
        [VMEM],
        [pltpu.VMEM(volume.shape, F32), pltpu.SemaphoreType.DMA((PARTS,))],
        outs_in=HBM,
    )(back)


def solution(mesh):
    in_specs = (P("chan", "depth", None), P(None, None, "chan", None, None), P(), P(), P())
    out_specs = P("chan", "depth", None)
    return jax.shard_map(
        per_device, mesh=mesh, in_specs=in_specs, out_specs=out_specs, check_vma=False
    )
```

```python
import functools

import jax
import jax.numpy as jnp
from jax import lax
from jax.experimental import pallas as pl
from jax.experimental.pallas import tpu as pltpu
from jax.sharding import PartitionSpec as P

W = 32
PARTS = 4
F32 = jnp.float32
BF16 = jnp.bfloat16
VMEM = pl.BlockSpec(memory_space=pltpu.VMEM)
HBM = pl.BlockSpec(memory_space=pltpu.HBM)


def call(body, outs, flops, moved, ins, scratch=(), aliases=None, outs_in=VMEM):
    return pl.pallas_call(
        body,
        out_shape=outs,
        in_specs=ins,
        out_specs=jax.tree.map(lambda _: outs_in, outs),
        scratch_shapes=scratch,
        input_output_aliases=aliases or {},
        cost_estimate=pl.CostEstimate(flops=flops, bytes_accessed=moved, transcendentals=0),
        compiler_params=pltpu.CompilerParams(vmem_limit_bytes=32 << 20),
    )


def halves(x):
    hi = x.astype(BF16)
    return hi, (x - hi.astype(F32)).astype(BF16)


def gelu(v):
    half = 0.5 * v
    slope = 0.7978845608028654
    return half + half * jnp.tanh(v * (slope + (0.044715 * slope) * (v * v)))


def turned_here():
    return lax.axis_index("depth") % 2 > 0


def rearranged(pieces, back):
    block = lax.broadcasted_iota(jnp.int32, pieces[0].shape, 1) // W
    count = len(pieces)
    runs = 128 // W
    moved = []
    for v in range(count):
        total = None
        for b in range(runs):
            if back:
                row = v * runs + b
                source, at = row % count, row // count
            else:
                row = b * count + v
                source, at = row // runs, row % runs
            piece = pieces[source]
            if at != b:
                piece = pltpu.roll(piece, (b - at) * W % 128, 1)
            total = piece if total is None else jnp.where(block == b, piece, total)
        moved.append(total)
    return moved


def first_plane_kernel(x_hbm, x_ref, q_ref, sems):
    rows = x_ref.shape[0] // PARTS
    copies = []
    for n in range(PARTS):
        part = pl.ds(n * rows, rows)
        copies.append(pltpu.make_async_copy(x_hbm.at[part], x_ref.at[part], sems.at[n]))
        copies[-1].start()
    for copy in copies:
        copy.wait()
    planes_kernel((0,), x_ref, q_ref)


def planes_kernel(places, x_ref, *q_refs):
    last = x_ref.shape[1] - 1
    flip = turned_here()
    for k, q_ref in zip(places, q_refs, strict=True):
        plane = jnp.where(flip, x_ref[:, last - k, :], x_ref[:, k, :])
        pieces = [plane[:, v : v + 128] for v in range(0, plane.shape[1], 128)]
        q_ref[...] = jnp.concatenate(rearranged(pieces, False), axis=1)


def taps_kernel(k_ref, w_ref, pad_ref):
    layers, width, taps = k_ref.shape
    flip = turned_here()
    lane = lax.broadcasted_iota(jnp.int32, (width, 128), 1)
    pad_ref[...] = jnp.zeros_like(pad_ref)
    for layer in range(layers):
        pad_ref[:, :taps] = k_ref[layer]
        for tap in range(9):
            start = tap * 3 * width
            base, shift = start // 128 * 128, start % 128
            pair = pad_ref[:, base : base + 256]
            if shift:
                pair = pltpu.roll(pair, 256 - shift, 1)
            ahead = pair[:, :128]
            turned = jnp.where(lane // width == 1, ahead, pltpu.roll(ahead, 2 * width, 1))
            hi, lo = halves(jnp.where(lane < 3 * width, jnp.where(flip, turned, ahead), 0.0))
            rows = pl.ds(tap * width, width)
            w_ref[layer, rows, 0:128] = hi
            w_ref[layer, rows, 128:256] = hi
            w_ref[layer, rows, 256:384] = lo


def first_weights_kernel(gain_ref, a_ref, w_ref):
    gain = gain_ref[...]
    hidden = a_ref.shape[0]
    rows = 128
    for r in range(0, hidden, rows):
        hi, lo = halves(a_ref[r : r + rows, :] * gain)
        w_ref[r : r + rows, :] = hi
        w_ref[hidden + r : hidden + r + rows, :] = lo


def second_weights_kernel(b_ref, w_ref):
    channels = b_ref.shape[0]
    rows = 128
    for r in range(0, channels, rows):
        hi, lo = halves(b_ref[r : r + rows, :])
        w_ref[r : r + rows, :] = hi
        w_ref[channels + r : channels + r + rows, :] = lo


def conv_plane(weight, three, acc_ref):
    zero = jnp.zeros_like(three[0][0])
    his = [t[0] for t in three] + [zero]
    los = [t[1] for t in three] + [zero]
    acc_ref[...] = jnp.dot(weight, jnp.concatenate(his + los + his, axis=0), preferred_element_type=F32)
    width, cells = zero.shape
    count = cells // 128

    def tap(b, c, v):
        return acc_ref[(b * 3 + c) * width : (b * 3 + c + 1) * width, v * 128 : (v + 1) * 128]

    def rows(c, v):
        above = tap(0, c, v - 1) if v else pltpu.roll(tap(0, c, count - 1), W, 1)
        below = tap(2, c, v + 1) if v < count - 1 else pltpu.roll(tap(2, c, 0), 128 - W, 1)
        return tap(1, c, v) + above + below

    column = lax.broadcasted_iota(jnp.int32, (width, 128), 1) % W
    parts = []
    for v in range(count):
        left, here, right = (rows(c, v) for c in range(3))
        left = jnp.where(column == 0, pltpu.roll(left, 128 - W + 1, 1), pltpu.roll(left, 1, 1))
        right = jnp.where(column == W - 1, pltpu.roll(right, W - 1, 1), pltpu.roll(right, 127, 1))
        parts.append(left + here + right)
    return jnp.concatenate(parts, axis=1)


def store_cells(out_ref, plane, value):
    size = out_ref.shape[2]
    runs = value.shape[1] // size
    for q in range(runs):
        out_ref[plane * runs + q] = value[:, q * size : (q + 1) * size]


def stage_kernel(given, work, kept, first, resumes, w_ref, *refs):
    ins, refs = refs[: len(given)], refs[len(given) :]
    acc_ref = refs[-1]
    layers = w_ref.shape[0]
    refs = refs[resumes:]
    where = dict(zip(given, ins, strict=True))
    kept_at = dict(zip(kept, refs[: len(kept)], strict=True))
    held = {key: halves(ref[...]) for key, ref in where.items()}
    for n, (layer, place) in enumerate(work):
        total = conv_plane(w_ref[layer - 1], [held[layer - 1, place + d] for d in (-1, 0, 1)], acc_ref.at[n % 2])
        if layer == layers:
            store_cells(refs[len(kept)], place - first, where[0, place][...] + total)
            continue
        total = gelu(total)
        held[layer, place] = halves(total)
        if (layer, place) in kept_at:
            kept_at[layer, place][...] = total


def mlp_kernel(y_ref, a_ref, b_ref, out_ref, hh_ref, hl_ref):
    channels = y_ref.shape[0]
    hidden = hh_ref.shape[0]
    rows = 256
    y = y_ref[...]
    scale = lax.rsqrt(jnp.mean(y * y, axis=0, keepdims=True) + 1e-06)
    hi, lo = halves(y * scale)
    seen = jnp.concatenate([hi, lo, hi], axis=0)
    for r in range(0, hidden, rows):
        top, low = a_ref[r : r + rows, :], a_ref[hidden + r : hidden + r + rows, :]
        hid = gelu(jnp.dot(jnp.concatenate([top, top, low], axis=1), seen, preferred_element_type=F32))
        hh, hl = halves(hid)
        hh_ref[r : r + rows, :] = hh
        hl_ref[r : r + rows, :] = hl
    seen = jnp.concatenate([hh_ref[...], hl_ref[...], hh_ref[...]], axis=0)
    for r in range(0, channels, rows):
        top, low = b_ref[r : r + rows, :], b_ref[channels + r : channels + r + rows, :]
        part = jnp.concatenate([top, top, low], axis=1)
        out_ref[r : r + rows, :] = y_ref[r : r + rows, :] + jnp.dot(part, seen, preferred_element_type=F32)


def place_kernel(in_ref, out_hbm, held_ref, sems):
    size = in_ref.shape[2]
    width, planes, cells = out_hbm.shape
    runs = cells // size
    flip = turned_here()
    rows = width // sems.shape[0]
    copies = []
    for n in range(width // rows):
        part = slice(n * rows, (n + 1) * rows)
        for p in range(planes):
            start = jnp.where(flip, planes - 1 - p, p) * runs
            pieces = [in_ref[start + q, part, v : v + 128] for q in range(runs) for v in range(0, size, 128)]
            for v, piece in enumerate(rearranged(pieces, True)):
                held_ref[part, p, v * 128 : (v + 1) * 128] = piece
        part = pl.ds(n * rows, rows)
        copies.append(pltpu.make_async_copy(held_ref.at[part], out_hbm.at[part], sems.at[n]))
        copies[-1].start()
    for copy in copies:
        copy.wait()


def per_device(volume, conv_weight, norm_gain, mlp_in, mlp_out):
    width, planes, cells = volume.shape
    count = lax.axis_size("depth")
    members = lax.axis_size("chan")
    kernels = conv_weight[0, :, 0]
    layers = kernels.shape[0]
    channels, hidden = mlp_out.shape[1], mlp_out.shape[2]
    size = planes * cells // members
    plane = jax.ShapeDtypeStruct((width, cells), F32)

    pair = [(i, i ^ 1) for i in range(count)]
    along = [(i, (i + (2 if i % 2 == 0 else count - 2)) % count) for i in range(count)]
    here, first = call(
        first_plane_kernel,
        (jax.ShapeDtypeStruct(volume.shape, F32), plane),
        10**9,
        volume.size * 8,
        [HBM],
        [pltpu.SemaphoreType.DMA((PARTS,))],
    )(pltpu.with_memory_space_constraint(volume, pltpu.HBM))
    body = functools.partial(planes_kernel, tuple(range(1, planes)))
    own = (first, *call(body, (plane,) * (planes - 1), 10**9, volume.size * 6, [VMEM])(here))
    there = [lax.ppermute(q, "depth", pair) for q in own[:2]]
    taps = call(
        taps_kernel,
        jax.ShapeDtypeStruct((layers, 9 * width, 384), BF16),
        0,
        kernels.size * 8,
        [VMEM],
        [pltpu.VMEM((width, 1024), F32)],
    )(kernels)
    held = {(0, 3 + k): v for k, v in enumerate(own)}

    def stage(given, work, kept, finished=None):
        outs = (plane,) * len(kept)
        if any(layer == layers for layer, _ in work):
            outs += (jax.ShapeDtypeStruct((members, width, size), F32),)
        more = [] if finished is None else [finished]
        got = call(
            functools.partial(stage_kernel, given, work, kept, layers, len(more)),
            outs,
            len(work) * 2 * 288 * 384 * cells,
            (len(given) + len(outs)) * width * cells * 4,
            [VMEM] * (1 + len(given) + len(more)),
            [pltpu.VMEM((2, 9 * width, cells), F32)],
            {1 + len(given): len(kept)} if more else None,
        )(taps, *[held[key] for key in given], *more)
        held.update(zip(kept, got))
        return got[-1]

    stage(((0, 3), (0, 4), (0, 5), (0, 6)), ((1, 4), (1, 5)), ((1, 4), (1, 5)))
    weights = jax.ShapeDtypeStruct((2 * hidden, channels), BF16)
    w_in = call(first_weights_kernel, weights, 0, mlp_in.size * 8, [VMEM] * 2)(norm_gain, mlp_in[0])
    third, held[1, 4], held[1, 5], w_in = lax.optimization_barrier((own[2], held[1, 4], held[1, 5], w_in))
    weights = jax.ShapeDtypeStruct((2 * channels, hidden), BF16)
    w_out = call(second_weights_kernel, weights, 0, mlp_out.size * 8, [VMEM])(mlp_out[0])
    fourth, w_out = lax.optimization_barrier((own[3], w_out))
    there[1], w_out = lax.optimization_barrier((there[1], w_out))
    there += [lax.ppermute(q, "depth", pair) for q in (third, fourth)]
    for k in range(layers):
        held[0, 2 - k] = lax.ppermute(there[k], "depth", along)
        held[0, 9 - k] = there[k + 1]
    stage(((0, 2), (0, 3), (0, 4), (1, 4), (1, 5)), ((1, 3), (2, 4)), ((1, 3), (2, 4)))
    most = stage(
        ((0, 5), (0, 6), (0, 7), (0, 8), (0, 9), (1, 4), (1, 5), (2, 4)),
        ((1, 6), (1, 7), (1, 8), (2, 5), (2, 6), (2, 7), (3, 5), (3, 6)),
        ((2, 5),),
    )
    mixed = stage(
        ((0, 0), (0, 1), (0, 2), (0, 3), (0, 4), (1, 3), (1, 4), (2, 4), (2, 5)),
        ((1, 2), (1, 1), (2, 3), (2, 2), (3, 4), (3, 3)),
        (),
        most,
    )
    here = lax.all_to_all(mixed, "chan", split_axis=0, concat_axis=0, tiled=True)
    out = call(
        mlp_kernel,
        jax.ShapeDtypeStruct((channels, size), F32),
        12 * hidden * channels * size,
        mlp_in.size * 8,
        [VMEM] * 3,
        [pltpu.VMEM((hidden, size), BF16)] * 2,
    )(here.reshape(channels, size), w_in, w_out)
    back = lax.all_to_all(out.reshape(members, width, size), "chan", split_axis=0, concat_axis=0, tiled=True)
    return call(
        place_kernel,
        jax.ShapeDtypeStruct(volume.shape, F32),
        0,
        volume.size * 8,
        [VMEM],
        [pltpu.VMEM(volume.shape, F32), pltpu.SemaphoreType.DMA((PARTS,))],
        outs_in=HBM,
    )(back)


def solution(mesh):
    in_specs = (P("chan", "depth", None), P(None, None, "chan", None, None), P(), P(), P())
    out_specs = P("chan", "depth", None)
    return jax.shard_map(
        per_device, mesh=mesh, in_specs=in_specs, out_specs=out_specs, check_vma=False
    )
```

```python
import functools

import jax
import jax.numpy as jnp
from jax import lax
from jax.experimental import pallas as pl
from jax.experimental.pallas import tpu as pltpu
from jax.sharding import PartitionSpec as P

W = 32
PARTS = 4
F32 = jnp.float32
BF16 = jnp.bfloat16
VMEM = pl.BlockSpec(memory_space=pltpu.VMEM)
HBM = pl.BlockSpec(memory_space=pltpu.HBM)


def call(body, outs, flops, moved, ins, scratch=(), aliases=None, outs_in=VMEM):
    return pl.pallas_call(
        body,
        out_shape=outs,
        in_specs=ins,
        out_specs=jax.tree.map(lambda _: outs_in, outs),
        scratch_shapes=scratch,
        input_output_aliases=aliases or {},
        cost_estimate=pl.CostEstimate(flops=flops, bytes_accessed=moved, transcendentals=0),
        compiler_params=pltpu.CompilerParams(vmem_limit_bytes=32 << 20),
    )


def halves(x):
    hi = x.astype(BF16)
    return hi, (x - hi.astype(F32)).astype(BF16)


def gelu(v):
    half = 0.5 * v
    slope = 0.7978845608028654
    return half + half * jnp.tanh(v * (slope + (0.044715 * slope) * (v * v)))


def turned_here():
    return lax.axis_index("depth") % 2 > 0


def rearranged(pieces, back):
    block = lax.broadcasted_iota(jnp.int32, pieces[0].shape, 1) // W
    count = len(pieces)
    runs = 128 // W
    moved = []
    for v in range(count):
        total = None
        for b in range(runs):
            if back:
                row = v * runs + b
                source, at = row % count, row // count
            else:
                row = b * count + v
                source, at = row // runs, row % runs
            piece = pieces[source]
            if at != b:
                piece = pltpu.roll(piece, (b - at) * W % 128, 1)
            total = piece if total is None else jnp.where(block == b, piece, total)
        moved.append(total)
    return moved


def first_plane_kernel(x_hbm, x_ref, q_ref, sems):
    rows = x_ref.shape[0] // PARTS
    copies = []
    for n in range(PARTS):
        part = pl.ds(n * rows, rows)
        copies.append(pltpu.make_async_copy(x_hbm.at[part], x_ref.at[part], sems.at[n]))
        copies[-1].start()
    for copy in copies:
        copy.wait()
    planes_kernel((0,), x_ref, q_ref)


def planes_kernel(places, x_ref, *q_refs):
    last = x_ref.shape[1] - 1
    flip = turned_here()
    for k, q_ref in zip(places, q_refs, strict=True):
        plane = jnp.where(flip, x_ref[:, last - k, :], x_ref[:, k, :])
        pieces = [plane[:, v : v + 128] for v in range(0, plane.shape[1], 128)]
        q_ref[...] = jnp.concatenate(rearranged(pieces, False), axis=1)


def taps_kernel(k_ref, w_ref, pad_ref):
    layers, width, taps = k_ref.shape
    flip = turned_here()
    lane = lax.broadcasted_iota(jnp.int32, (width, 128), 1)
    pad_ref[...] = jnp.zeros_like(pad_ref)
    for layer in range(layers):
        pad_ref[:, :taps] = k_ref[layer]
        for tap in range(9):
            start = tap * 3 * width
            base, shift = start // 128 * 128, start % 128
            pair = pad_ref[:, base : base + 256]
            if shift:
                pair = pltpu.roll(pair, 256 - shift, 1)
            ahead = pair[:, :128]
            turned = jnp.where(lane // width == 1, ahead, pltpu.roll(ahead, 2 * width, 1))
            hi, lo = halves(jnp.where(lane < 3 * width, jnp.where(flip, turned, ahead), 0.0))
            rows = pl.ds(tap * width, width)
            w_ref[layer, rows, 0:128] = hi
            w_ref[layer, rows, 128:256] = hi
            w_ref[layer, rows, 256:384] = lo


def first_weights_kernel(gain_ref, a_ref, w_ref):
    gain = gain_ref[...]
    hidden = a_ref.shape[0]
    rows = 128
    for r in range(0, hidden, rows):
        hi, lo = halves(a_ref[r : r + rows, :] * gain)
        w_ref[r : r + rows, :] = hi
        w_ref[hidden + r : hidden + r + rows, :] = lo


def second_weights_kernel(b_ref, w_ref):
    channels = b_ref.shape[0]
    rows = 128
    for r in range(0, channels, rows):
        hi, lo = halves(b_ref[r : r + rows, :])
        w_ref[r : r + rows, :] = hi
        w_ref[channels + r : channels + r + rows, :] = lo


def conv_plane(weight, three, acc_ref):
    zero = jnp.zeros_like(three[0][0])
    his = [t[0] for t in three] + [zero]
    los = [t[1] for t in three] + [zero]
    acc_ref[...] = jnp.dot(weight, jnp.concatenate(his + los + his, axis=0), preferred_element_type=F32)
    width, cells = zero.shape
    count = cells // 128

    def tap(b, c, v):
        return acc_ref[(b * 3 + c) * width : (b * 3 + c + 1) * width, v * 128 : (v + 1) * 128]

    def rows(c, v):
        above = tap(0, c, v - 1) if v else pltpu.roll(tap(0, c, count - 1), W, 1)
        below = tap(2, c, v + 1) if v < count - 1 else pltpu.roll(tap(2, c, 0), 128 - W, 1)
        return tap(1, c, v) + above + below

    column = lax.broadcasted_iota(jnp.int32, (width, 128), 1) % W
    parts = []
    for v in range(count):
        left, here, right = (rows(c, v) for c in range(3))
        left = jnp.where(column == 0, pltpu.roll(left, 128 - W + 1, 1), pltpu.roll(left, 1, 1))
        right = jnp.where(column == W - 1, pltpu.roll(right, W - 1, 1), pltpu.roll(right, 127, 1))
        parts.append(left + here + right)
    return jnp.concatenate(parts, axis=1)


def store_cells(out_ref, plane, value):
    size = out_ref.shape[2]
    runs = value.shape[1] // size
    for q in range(runs):
        out_ref[plane * runs + q] = value[:, q * size : (q + 1) * size]


def stage_kernel(given, work, kept, first, resumes, w_ref, *refs):
    ins, refs = refs[: len(given)], refs[len(given) :]
    acc_ref = refs[-1]
    layers = w_ref.shape[0]
    refs = refs[resumes:]
    where = dict(zip(given, ins, strict=True))
    kept_at = dict(zip(kept, refs[: len(kept)], strict=True))
    width = w_ref.shape[1] // 9
    held = {key: (ref[:width], ref[width:]) if key[0] else halves(ref[...]) for key, ref in where.items()}
    for n, (layer, place) in enumerate(work):
        total = conv_plane(w_ref[layer - 1], [held[layer - 1, place + d] for d in (-1, 0, 1)], acc_ref.at[n % 2])
        if layer == layers:
            store_cells(refs[len(kept)], place - first, where[0, place][...] + total)
            continue
        hi, lo = halves(gelu(total))
        held[layer, place] = hi, lo
        if (layer, place) in kept_at:
            kept_at[layer, place][:width] = hi
            kept_at[layer, place][width:] = lo


def mlp_kernel(y_ref, a_ref, b_ref, out_ref, hh_ref, hl_ref):
    channels = y_ref.shape[0]
    hidden = hh_ref.shape[0]
    rows = 256
    y = y_ref[...]
    scale = lax.rsqrt(jnp.mean(y * y, axis=0, keepdims=True) + 1e-06)
    hi, lo = halves(y * scale)
    seen = jnp.concatenate([hi, lo, hi], axis=0)
    for r in range(0, hidden, rows):
        top, low = a_ref[r : r + rows, :], a_ref[hidden + r : hidden + r + rows, :]
        hid = gelu(jnp.dot(jnp.concatenate([top, top, low], axis=1), seen, preferred_element_type=F32))
        hh, hl = halves(hid)
        hh_ref[r : r + rows, :] = hh
        hl_ref[r : r + rows, :] = hl
    seen = jnp.concatenate([hh_ref[...], hl_ref[...], hh_ref[...]], axis=0)
    for r in range(0, channels, rows):
        top, low = b_ref[r : r + rows, :], b_ref[channels + r : channels + r + rows, :]
        part = jnp.concatenate([top, top, low], axis=1)
        out_ref[r : r + rows, :] = y_ref[r : r + rows, :] + jnp.dot(part, seen, preferred_element_type=F32)


def place_kernel(in_ref, out_hbm, held_ref, sems):
    size = in_ref.shape[2]
    width, planes, cells = out_hbm.shape
    runs = cells // size
    flip = turned_here()
    rows = width // sems.shape[0]
    copies = []
    for n in range(width // rows):
        part = slice(n * rows, (n + 1) * rows)
        for p in range(planes):
            start = jnp.where(flip, planes - 1 - p, p) * runs
            pieces = [in_ref[start + q, part, v : v + 128] for q in range(runs) for v in range(0, size, 128)]
            for v, piece in enumerate(rearranged(pieces, True)):
                held_ref[part, p, v * 128 : (v + 1) * 128] = piece
        part = pl.ds(n * rows, rows)
        copies.append(pltpu.make_async_copy(held_ref.at[part], out_hbm.at[part], sems.at[n]))
        copies[-1].start()
    for copy in copies:
        copy.wait()


def per_device(volume, conv_weight, norm_gain, mlp_in, mlp_out):
    width, planes, cells = volume.shape
    count = lax.axis_size("depth")
    members = lax.axis_size("chan")
    kernels = conv_weight[0, :, 0]
    layers = kernels.shape[0]
    channels, hidden = mlp_out.shape[1], mlp_out.shape[2]
    size = planes * cells // members
    plane = jax.ShapeDtypeStruct((width, cells), F32)

    pair = [(i, i ^ 1) for i in range(count)]
    along = [(i, (i + (2 if i % 2 == 0 else count - 2)) % count) for i in range(count)]
    here, first = call(
        first_plane_kernel,
        (jax.ShapeDtypeStruct(volume.shape, F32), plane),
        10**9,
        volume.size * 8,
        [HBM],
        [pltpu.SemaphoreType.DMA((PARTS,))],
    )(pltpu.with_memory_space_constraint(volume, pltpu.HBM))
    body = functools.partial(planes_kernel, tuple(range(1, planes)))
    own = (first, *call(body, (plane,) * (planes - 1), 10**9, volume.size * 6, [VMEM])(here))
    there = [lax.ppermute(q, "depth", pair) for q in own[:2]]
    taps = call(
        taps_kernel,
        jax.ShapeDtypeStruct((layers, 9 * width, 384), BF16),
        0,
        kernels.size * 8,
        [VMEM],
        [pltpu.VMEM((width, 1024), F32)],
    )(kernels)
    held = {(0, 3 + k): v for k, v in enumerate(own)}

    def stage(given, work, kept, finished=None):
        outs = (jax.ShapeDtypeStruct((2 * width, cells), BF16),) * len(kept)
        if any(layer == layers for layer, _ in work):
            outs += (jax.ShapeDtypeStruct((members, width, size), F32),)
        more = [] if finished is None else [finished]
        got = call(
            functools.partial(stage_kernel, given, work, kept, layers, len(more)),
            outs,
            len(work) * 2 * 288 * 384 * cells,
            (len(given) + len(outs)) * width * cells * 4,
            [VMEM] * (1 + len(given) + len(more)),
            [pltpu.VMEM((2, 9 * width, cells), F32)],
            {1 + len(given): len(kept)} if more else None,
        )(taps, *[held[key] for key in given], *more)
        held.update(zip(kept, got))
        return got[-1]

    stage(((0, 3), (0, 4), (0, 5), (0, 6)), ((1, 4), (1, 5)), ((1, 4), (1, 5)))
    weights = jax.ShapeDtypeStruct((2 * hidden, channels), BF16)
    w_in = call(first_weights_kernel, weights, 0, mlp_in.size * 8, [VMEM] * 2)(norm_gain, mlp_in[0])
    third, held[1, 4], held[1, 5], w_in = lax.optimization_barrier((own[2], held[1, 4], held[1, 5], w_in))
    weights = jax.ShapeDtypeStruct((2 * channels, hidden), BF16)
    w_out = call(second_weights_kernel, weights, 0, mlp_out.size * 8, [VMEM])(mlp_out[0])
    fourth, w_out = lax.optimization_barrier((own[3], w_out))
    there[1], w_out = lax.optimization_barrier((there[1], w_out))
    there += [lax.ppermute(q, "depth", pair) for q in (third, fourth)]
    for k in range(layers):
        held[0, 2 - k] = lax.ppermute(there[k], "depth", along)
        held[0, 9 - k] = there[k + 1]
    stage(((0, 2), (0, 3), (0, 4), (1, 4), (1, 5)), ((1, 3), (2, 4)), ((1, 3), (2, 4)))
    most = stage(
        ((0, 5), (0, 6), (0, 7), (0, 8), (0, 9), (1, 4), (1, 5), (2, 4)),
        ((1, 6), (1, 7), (1, 8), (2, 5), (2, 6), (2, 7), (3, 5), (3, 6)),
        ((2, 5),),
    )
    mixed = stage(
        ((0, 0), (0, 1), (0, 2), (0, 3), (0, 4), (1, 3), (1, 4), (2, 4), (2, 5)),
        ((1, 2), (1, 1), (2, 3), (2, 2), (3, 4), (3, 3)),
        (),
        most,
    )
    here = lax.all_to_all(mixed, "chan", split_axis=0, concat_axis=0, tiled=True)
    out = call(
        mlp_kernel,
        jax.ShapeDtypeStruct((channels, size), F32),
        12 * hidden * channels * size,
        mlp_in.size * 8,
        [VMEM] * 3,
        [pltpu.VMEM((hidden, size), BF16)] * 2,
    )(here.reshape(channels, size), w_in, w_out)
    back = lax.all_to_all(out.reshape(members, width, size), "chan", split_axis=0, concat_axis=0, tiled=True)
    return call(
        place_kernel,
        jax.ShapeDtypeStruct(volume.shape, F32),
        0,
        volume.size * 8,
        [VMEM],
        [pltpu.VMEM(volume.shape, F32), pltpu.SemaphoreType.DMA((PARTS,))],
        outs_in=HBM,
    )(back)


def solution(mesh):
    in_specs = (P("chan", "depth", None), P(None, None, "chan", None, None), P(), P(), P())
    out_specs = P("chan", "depth", None)
    return jax.shard_map(
        per_device, mesh=mesh, in_specs=in_specs, out_specs=out_specs, check_vma=False
    )
```

```python
import functools

import jax
import jax.numpy as jnp
from jax import lax
from jax.experimental import pallas as pl
from jax.experimental.pallas import tpu as pltpu
from jax.sharding import PartitionSpec as P

W = 32
PARTS = 4
F32 = jnp.float32
BF16 = jnp.bfloat16
VMEM = pl.BlockSpec(memory_space=pltpu.VMEM)
HBM = pl.BlockSpec(memory_space=pltpu.HBM)


def call(body, outs, flops, moved, ins, scratch=(), aliases=None, outs_in=VMEM):
    return pl.pallas_call(
        body,
        out_shape=outs,
        in_specs=ins,
        out_specs=jax.tree.map(lambda _: outs_in, outs),
        scratch_shapes=scratch,
        input_output_aliases=aliases or {},
        cost_estimate=pl.CostEstimate(flops=flops, bytes_accessed=moved, transcendentals=0),
        compiler_params=pltpu.CompilerParams(vmem_limit_bytes=32 << 20),
    )


def halves(x):
    hi = x.astype(BF16)
    return hi, (x - hi.astype(F32)).astype(BF16)


def gelu(v):
    half = 0.5 * v
    slope = 0.7978845608028654
    return half + half * jnp.tanh(v * (slope + (0.044715 * slope) * (v * v)))


def turned_here():
    return lax.axis_index("depth") % 2 > 0


def rearranged(pieces, back):
    block = lax.broadcasted_iota(jnp.int32, pieces[0].shape, 1) // W
    count = len(pieces)
    runs = 128 // W
    moved = []
    for v in range(count):
        total = None
        for b in range(runs):
            if back:
                row = v * runs + b
                source, at = row % count, row // count
            else:
                row = b * count + v
                source, at = row // runs, row % runs
            piece = pieces[source]
            if at != b:
                piece = pltpu.roll(piece, (b - at) * W % 128, 1)
            total = piece if total is None else jnp.where(block == b, piece, total)
        moved.append(total)
    return moved


def planes_kernel(places, x_ref, *q_refs):
    last = x_ref.shape[1] - 1
    flip = turned_here()
    for k, q_ref in zip(places, q_refs, strict=True):
        plane = jnp.where(flip, x_ref[:, last - k, :], x_ref[:, k, :])
        pieces = [plane[:, v : v + 128] for v in range(0, plane.shape[1], 128)]
        q_ref[...] = jnp.concatenate(rearranged(pieces, False), axis=1)


def taps_kernel(k_ref, w_ref, pad_ref):
    layers, width, taps = k_ref.shape
    flip = turned_here()
    lane = lax.broadcasted_iota(jnp.int32, (width, 128), 1)
    pad_ref[...] = jnp.zeros_like(pad_ref)
    for layer in range(layers):
        pad_ref[:, :taps] = k_ref[layer]
        for tap in range(9):
            start = tap * 3 * width
            base, shift = start // 128 * 128, start % 128
            pair = pad_ref[:, base : base + 256]
            if shift:
                pair = pltpu.roll(pair, 256 - shift, 1)
            ahead = pair[:, :128]
            turned = jnp.where(lane // width == 1, ahead, pltpu.roll(ahead, 2 * width, 1))
            hi, lo = halves(jnp.where(lane < 3 * width, jnp.where(flip, turned, ahead), 0.0))
            rows = pl.ds(tap * width, width)
            w_ref[layer, rows, 0:128] = hi
            w_ref[layer, rows, 128:256] = hi
            w_ref[layer, rows, 256:384] = lo


def first_weights_kernel(gain_ref, a_ref, w_ref):
    gain = gain_ref[...]
    hidden = a_ref.shape[0]
    rows = 128
    for r in range(0, hidden, rows):
        hi, lo = halves(a_ref[r : r + rows, :] * gain)
        w_ref[r : r + rows, :] = hi
        w_ref[hidden + r : hidden + r + rows, :] = lo


def second_weights_kernel(b_ref, w_ref):
    channels = b_ref.shape[0]
    rows = 128
    for r in range(0, channels, rows):
        hi, lo = halves(b_ref[r : r + rows, :])
        w_ref[r : r + rows, :] = hi
        w_ref[channels + r : channels + r + rows, :] = lo


def conv_plane(weight, three, acc_ref):
    zero = jnp.zeros_like(three[0][0])
    his = [t[0] for t in three] + [zero]
    los = [t[1] for t in three] + [zero]
    acc_ref[...] = jnp.dot(weight, jnp.concatenate(his + los + his, axis=0), preferred_element_type=F32)
    width, cells = zero.shape
    count = cells // 128

    def tap(b, c, v):
        return acc_ref[(b * 3 + c) * width : (b * 3 + c + 1) * width, v * 128 : (v + 1) * 128]

    def rows(c, v):
        above = tap(0, c, v - 1) if v else pltpu.roll(tap(0, c, count - 1), W, 1)
        below = tap(2, c, v + 1) if v < count - 1 else pltpu.roll(tap(2, c, 0), 128 - W, 1)
        return tap(1, c, v) + above + below

    column = lax.broadcasted_iota(jnp.int32, (width, 128), 1) % W
    parts = []
    for v in range(count):
        left, here, right = (rows(c, v) for c in range(3))
        left = jnp.where(column == 0, pltpu.roll(left, 128 - W + 1, 1), pltpu.roll(left, 1, 1))
        right = jnp.where(column == W - 1, pltpu.roll(right, W - 1, 1), pltpu.roll(right, 127, 1))
        parts.append(left + here + right)
    return jnp.concatenate(parts, axis=1)


def store_cells(out_ref, plane, value):
    size = out_ref.shape[2]
    runs = value.shape[1] // size
    for q in range(runs):
        out_ref[plane * runs + q] = value[:, q * size : (q + 1) * size]


def stage_kernel(given, work, kept, first, resumes, w_ref, *refs):
    ins, refs = refs[: len(given)], refs[len(given) :]
    acc_ref = refs[-1]
    layers = w_ref.shape[0]
    refs = refs[resumes:]
    where = dict(zip(given, ins, strict=True))
    kept_at = dict(zip(kept, refs[: len(kept)], strict=True))
    held = {key: halves(ref[...]) for key, ref in where.items()}
    for n, (layer, place) in enumerate(work):
        total = conv_plane(w_ref[layer - 1], [held[layer - 1, place + d] for d in (-1, 0, 1)], acc_ref.at[n % 2])
        if layer == layers:
            store_cells(refs[len(kept)], place - first, where[0, place][...] + total)
            continue
        total = gelu(total)
        held[layer, place] = halves(total)
        if (layer, place) in kept_at:
            kept_at[layer, place][...] = total


def mlp_kernel(y_ref, a_ref, b_ref, out_ref, hh_ref, hl_ref):
    channels = y_ref.shape[0]
    hidden = hh_ref.shape[0]
    rows = 256
    y = y_ref[...]
    scale = lax.rsqrt(jnp.mean(y * y, axis=0, keepdims=True) + 1e-06)
    hi, lo = halves(y * scale)
    seen = jnp.concatenate([hi, lo, hi], axis=0)
    for r in range(0, hidden, rows):
        top, low = a_ref[r : r + rows, :], a_ref[hidden + r : hidden + r + rows, :]
        hid = gelu(jnp.dot(jnp.concatenate([top, top, low], axis=1), seen, preferred_element_type=F32))
        hh, hl = halves(hid)
        hh_ref[r : r + rows, :] = hh
        hl_ref[r : r + rows, :] = hl
    seen = jnp.concatenate([hh_ref[...], hl_ref[...], hh_ref[...]], axis=0)
    for r in range(0, channels, rows):
        top, low = b_ref[r : r + rows, :], b_ref[channels + r : channels + r + rows, :]
        part = jnp.concatenate([top, top, low], axis=1)
        out_ref[r : r + rows, :] = y_ref[r : r + rows, :] + jnp.dot(part, seen, preferred_element_type=F32)


def place_kernel(in_ref, out_hbm, held_ref, sems):
    size = in_ref.shape[2]
    width, planes, cells = out_hbm.shape
    runs = cells // size
    flip = turned_here()
    rows = width // sems.shape[0]
    copies = []
    for n in range(width // rows):
        part = slice(n * rows, (n + 1) * rows)
        for p in range(planes):
            start = jnp.where(flip, planes - 1 - p, p) * runs
            pieces = [in_ref[start + q, part, v : v + 128] for q in range(runs) for v in range(0, size, 128)]
            for v, piece in enumerate(rearranged(pieces, True)):
                held_ref[part, p, v * 128 : (v + 1) * 128] = piece
        part = pl.ds(n * rows, rows)
        copies.append(pltpu.make_async_copy(held_ref.at[part], out_hbm.at[part], sems.at[n]))
        copies[-1].start()
    for copy in copies:
        copy.wait()


def per_device(volume, conv_weight, norm_gain, mlp_in, mlp_out):
    width, planes, cells = volume.shape
    count = lax.axis_size("depth")
    members = lax.axis_size("chan")
    kernels = conv_weight[0, :, 0]
    layers = kernels.shape[0]
    channels, hidden = mlp_out.shape[1], mlp_out.shape[2]
    size = planes * cells // members
    plane = jax.ShapeDtypeStruct((width, cells), F32)

    pair = [(i, i ^ 1) for i in range(count)]
    along = [(i, (i + (2 if i % 2 == 0 else count - 2)) % count) for i in range(count)]
    own = []
    for places in ((0,), tuple(range(1, planes))):
        body = functools.partial(planes_kernel, places)
        own += call(body, (plane,) * len(places), 10**9, len(places) * width * cells * 8, [VMEM])(volume)
    there = [lax.ppermute(q, "depth", pair) for q in own[:2]]
    taps = call(
        taps_kernel,
        jax.ShapeDtypeStruct((layers, 9 * width, 384), BF16),
        0,
        kernels.size * 8,
        [VMEM],
        [pltpu.VMEM((width, 1024), F32)],
    )(kernels)
    held = {(0, 3 + k): v for k, v in enumerate(own)}

    def stage(given, work, kept, finished=None):
        outs = (plane,) * len(kept)
        if any(layer == layers for layer, _ in work):
            outs += (jax.ShapeDtypeStruct((members, width, size), F32),)
        more = [] if finished is None else [finished]
        got = call(
            functools.partial(stage_kernel, given, work, kept, layers, len(more)),
            outs,
            len(work) * 2 * 288 * 384 * cells,
            (len(given) + len(outs)) * width * cells * 4,
            [VMEM] * (1 + len(given) + len(more)),
            [pltpu.VMEM((2, 9 * width, cells), F32)],
            {1 + len(given): len(kept)} if more else None,
        )(taps, *[held[key] for key in given], *more)
        held.update(zip(kept, got))
        return got[-1]

    stage(((0, 3), (0, 4), (0, 5), (0, 6)), ((1, 4), (1, 5)), ((1, 4), (1, 5)))
    weights = jax.ShapeDtypeStruct((2 * hidden, channels), BF16)
    w_in = call(first_weights_kernel, weights, 0, mlp_in.size * 8, [VMEM] * 2)(norm_gain, mlp_in[0])
    third, held[1, 4], held[1, 5], w_in = lax.optimization_barrier((own[2], held[1, 4], held[1, 5], w_in))
    weights = jax.ShapeDtypeStruct((2 * channels, hidden), BF16)
    w_out = call(second_weights_kernel, weights, 0, mlp_out.size * 8, [VMEM])(mlp_out[0])
    fourth, w_out = lax.optimization_barrier((own[3], w_out))
    there[1], w_out = lax.optimization_barrier((there[1], w_out))
    there += [lax.ppermute(q, "depth", pair) for q in (third, fourth)]
    for k in range(layers):
        held[0, 2 - k] = lax.ppermute(there[k], "depth", along)
        held[0, 9 - k] = there[k + 1]
    stage(((0, 2), (0, 3), (0, 4), (1, 4), (1, 5)), ((1, 3), (2, 4)), ((1, 3), (2, 4)))
    most = stage(
        ((0, 5), (0, 6), (0, 7), (0, 8), (0, 9), (1, 4), (1, 5), (2, 4)),
        ((1, 6), (1, 7), (1, 8), (2, 5), (2, 6), (2, 7), (3, 5), (3, 6)),
        ((2, 5),),
    )
    mixed = stage(
        ((0, 0), (0, 1), (0, 2), (0, 3), (0, 4), (1, 3), (1, 4), (2, 4), (2, 5)),
        ((1, 2), (1, 1), (2, 3), (2, 2), (3, 4), (3, 3)),
        (),
        most,
    )
    here = lax.all_to_all(mixed, "chan", split_axis=0, concat_axis=0, tiled=True)
    out = call(
        mlp_kernel,
        jax.ShapeDtypeStruct((channels, size), F32),
        12 * hidden * channels * size,
        mlp_in.size * 8,
        [VMEM] * 3,
        [pltpu.VMEM((hidden, size), BF16)] * 2,
    )(here.reshape(channels, size), w_in, w_out)
    back = lax.all_to_all(out.reshape(members, width, size), "chan", split_axis=0, concat_axis=0, tiled=True)
    return call(
        place_kernel,
        jax.ShapeDtypeStruct(volume.shape, F32),
        0,
        volume.size * 8,
        [VMEM],
        [pltpu.VMEM(volume.shape, F32), pltpu.SemaphoreType.DMA((PARTS,))],
        outs_in=HBM,
    )(back)


def solution(mesh):
    in_specs = (P("chan", "depth", None), P(None, None, "chan", None, None), P(), P(), P())
    out_specs = P("chan", "depth", None)
    return jax.shard_map(
        per_device, mesh=mesh, in_specs=in_specs, out_specs=out_specs, check_vma=False
    )
```
